128 devices in a mesh: pipe: 2 (over y_lo), ctx: 16 (over y_hi, x, core), tp: 4 (over z).
Axes of the slice: x: 4, y: 4 (y_hi: 2, y_lo: 2; y = y_hi * 2 + y_lo), z: 4, core: 2. Of those that a mesh axis runs over, the one named last changes fastest.
Arguments:
- queries: bfloat16 [2, 8192, 4096], P('pipe', 'ctx', 'tp'), may hold values from -24 to 24
- keys: bfloat16 [2, 8192, 4096], P('pipe', 'ctx', 'tp'), may hold values from -24 to 24
- values: bfloat16 [2, 8192, 4096], P('pipe', 'ctx', 'tp'), may hold values from -6 to 6
- stream: bfloat16 [2, 8192, 8192], P('pipe', 'ctx', 'tp'), may hold values from -6 to 6
- grad_stream: bfloat16 [2, 8192, 8192], P('pipe', 'ctx', 'tp'), may hold values from -6 to 6
- out_proj: bfloat16 [2, 4096, 8192], P('pipe', 'tp'), may hold values from -0.09375 to 0.09375
- doc_ids: int32 [2, 8192], P('pipe'), may hold values from 0 to 7, never falling along the last dimension, each value on 1 to 1536 neighbouring positions
Outputs:
- grad_queries: bfloat16 [2, 8192, 4096], P('pipe', 'ctx', 'tp')
- grad_keys: bfloat16 [2, 8192, 4096], P('pipe', 'ctx', 'tp')
- grad_values: bfloat16 [2, 8192, 4096], P('pipe', 'ctx', 'tp')
- next_stream: bfloat16 [2, 8192, 8192], P('pipe', 'ctx', 'tp')
- next_grad: bfloat16 [2, 8192, 8192], P('pipe', 'ctx', 'tp')
The draws below stay inside these ranges and needn't reach their ends.
Inputs may be any that keep to these rules, and one draw needn't show every extreme that they name: `doc_ids`: document numbers never fall along a micro-batch; a document has at most 1536 tokens.
All inputs are finite; a program needn't handle non-finite values.
Results may differ from the reference program's by a relative error of at most 0.02.
Values may be sent and summed in bfloat16 or wider, within the bound.
A program may use at most 192 MiB of HBM per device.

```python
import math
import jax
import jax.numpy as jnp
import numpy as np
from jax import lax

D = 8192
HL = 8
HD = 128
TOK_DEV = 512
HEADS = 32
SECTIONS = 2
TOKENS = 8192
WINDOW = 512
DOCS = 8


def paired_parts(key):
    shape = (SECTIONS, TOKENS // 2, 2, HEADS, HD)
    base = jnp.clip(jax.random.normal(jax.random.fold_in(key, 11), shape, jnp.float32), -4.0, 4.0)
    second = jnp.clip(jax.random.normal(jax.random.fold_in(key, 12), shape, jnp.float32), -4.0, 4.0)
    return (base, second)


def draw_queries(key, part):
    base, second = paired_parts(key)
    result = base
    return result.reshape(SECTIONS, TOKENS, HEADS * HD).astype(jnp.bfloat16)


def draw_keys(key, part):
    base, second = paired_parts(key)
    result = second
    return result.reshape(SECTIONS, TOKENS, HEADS * HD).astype(jnp.bfloat16)


def block_levels(stream_key, dims, shards, low, largest):
    def one(dim, parts):
        heights = jax.random.uniform(jax.random.fold_in(jax.random.fold_in(stream_key, 6), dim), (parts,), jnp.float32, low / len(shards), largest / len(shards))
        return jnp.repeat(jnp.exp(heights), dims[dim] // parts).reshape((-1,) + (1,) * (len(dims) - dim - 1))

    gain = one(*shards[0])
    for cut in shards[1:]:
        gain = gain * one(*cut)
    return gain


def split_up(count, total, bound, slope):
    loads = [(1 << 20) // math.isqrt(grade ** slope) + 1 for grade in range(2, count + 1)]
    rest, given = total - bound - (count - 1), [1] * (count - 1)
    while rest > 0:
        movable = [i for i in range(count - 1) if given[i] < bound]
        mass, remaining = sum([loads[i] for i in movable]), rest
        for i in movable:
            addition = min(bound - given[i], max(1, remaining * loads[i] // mass), rest)
            given[i] = given[i] + addition
            rest = rest - addition
    return np.array([bound] + given)


def ragged(rng, count, total, bound, slope):
    if count == 2:
        one = jax.random.randint(rng, (), max(1, total - bound), min(bound, total - 1) + 1)
        return jnp.stack([one, total - one])
    lengths = jnp.asarray(split_up(count, total, bound, slope), jnp.int32)
    couples = (count - 1) // 2
    giver, taker = lengths[1:1 + 2 * couples:2], lengths[2:2 + 2 * couples:2]
    slack = jnp.minimum(giver - 1, bound - taker)
    passed = jax.random.randint(jax.random.fold_in(rng, 1), (couples,), 0, 1 << 20) % (slack + 1)
    lengths = lengths.at[1:1 + 2 * couples:2].set(giver - passed).at[2:2 + 2 * couples:2].set(taker + passed)
    return lengths[jax.random.permutation(jax.random.fold_in(rng, 2), count)]


def bell_draw(key, shape, width, most, split=(), kind=jnp.bfloat16):
    values = jax.random.normal(key, shape, jnp.float32) * width
    if len(split) > 0:
        values = block_levels(key, shape, split, -0.22, 0.18) * values
    return jnp.clip(values, min=-most, max=most).astype(kind)


def setup_inputs(seed: int = 0) -> dict:
    key_of = jax.random.split(jax.random.key(seed), 8)
    return {
        "queries": draw_queries(jax.random.fold_in(key_of[7], 71), 0),
        "keys": draw_keys(jax.random.fold_in(key_of[7], 71), 0),
        "values": bell_draw(key_of[2], (SECTIONS, TOKENS, HEADS * HD), 1.0, 6.0, ((0, 2), (1, 16), (2, 4))),
        "stream": bell_draw(key_of[3], (SECTIONS, TOKENS, D), 1.0, 6.0, ((0, 2), (1, 16), (2, 4))),
        "grad_stream": bell_draw(key_of[4], (SECTIONS, TOKENS, D), 1.0, 6.0, ((0, 2), (1, 16), (2, 4))),
        "out_proj": bell_draw(key_of[5], (SECTIONS, HEADS * HD, D), (HEADS * HD) ** -0.5, 0.09375, ((0, 2), (1, 4))),
        "doc_ids": jax.vmap(lambda own: jnp.searchsorted(jnp.cumsum(ragged(own, DOCS, TOKENS, 3 * TOK_DEV, 0)), jnp.arange(TOKENS), side="right"))(jax.random.split(key_of[6], SECTIONS)).reshape((SECTIONS, TOKENS)).astype(jnp.int32),
    }


NEG = -1.0e30


def block_terms(query_block, key_block, value_block, dout_block, visible):
    scaling = HD ** -0.5
    query_wide = query_block.astype(jnp.float32)
    key_wide = key_block.astype(jnp.float32)
    value_wide = value_block.astype(jnp.float32)
    dout_wide = dout_block.astype(jnp.float32)
    scores = jnp.einsum("qhd,khd->hqk", query_wide, key_wide) * scaling
    masked = jnp.where(visible[None], scores, NEG)
    row_max = jnp.max(masked, axis=-1, keepdims=True)
    exponent = jnp.where(visible[None], jnp.exp(masked - row_max), 0.0)
    row_sum = jnp.sum(exponent, axis=-1, keepdims=True)
    probability = exponent / row_sum
    weights = probability.astype(jnp.bfloat16)
    weights_wide = weights.astype(jnp.float32)
    attended = jnp.einsum("hqk,khd->qhd", weights_wide, value_wide).astype(jnp.bfloat16)
    row_delta = jnp.einsum("qhd,qhd->hq", dout_wide, attended.astype(jnp.float32))[..., None]
    d_prob = jnp.einsum("qhd,khd->hqk", dout_wide, value_wide)
    d_score = (probability * (d_prob - row_delta)).astype(jnp.bfloat16).astype(jnp.float32)
    d_value = jnp.einsum("hqk,qhd->khd", weights_wide, dout_wide)
    d_query = (jnp.einsum("hqk,khd->qhd", d_score, key_wide) * scaling).astype(jnp.bfloat16)
    d_key = jnp.einsum("hqk,qhd->khd", d_score, query_wide) * scaling
    return attended, d_query, d_key, d_value


def one_section(queries, keys, values, stream, grad_stream, out_proj, doc_ids):
    blocks = TOKENS // TOK_DEV
    feature = queries.shape[1]
    head_count = feature // HD
    d_out = lax.dot_general(grad_stream, out_proj, (((1,), (1,)), ((), ())), preferred_element_type=jnp.float32).astype(jnp.bfloat16)

    def to_blocks(array):
        return array.reshape(blocks, TOK_DEV, head_count, HD)

    zero_block = jnp.zeros((1, TOK_DEV, head_count, HD), jnp.bfloat16)
    key_pad = jnp.concatenate([zero_block, to_blocks(keys)], 0)
    value_pad = jnp.concatenate([zero_block, to_blocks(values)], 0)
    key_pairs = jnp.concatenate([key_pad[:-1], key_pad[1:]], 1)
    value_pairs = jnp.concatenate([value_pad[:-1], value_pad[1:]], 1)
    doc_blocks = doc_ids.reshape(blocks, TOK_DEV).astype(jnp.int32)
    doc_pad = jnp.concatenate([jnp.full((1, TOK_DEV), -1, jnp.int32), doc_blocks], 0)
    key_docs = jnp.concatenate([doc_pad[:-1], doc_pad[1:]], 1)
    block_index = jnp.arange(blocks, dtype=jnp.int32)

    def block_step(block_item):
        query_block, key_block, value_block, dout_block, query_doc, key_doc, position = block_item
        query_pos = position * TOK_DEV + jnp.arange(TOK_DEV, dtype=jnp.int32)
        key_pos = (position - 1) * TOK_DEV + jnp.arange(2 * TOK_DEV, dtype=jnp.int32)
        visible = (key_pos[None, :] <= query_pos[:, None]) & (query_pos[:, None] - key_pos[None, :] < WINDOW)
        visible = visible & (key_pos[None, :] >= 0) & (key_doc[None, :] == query_doc[:, None])
        return block_terms(query_block, key_block, value_block, dout_block, visible)

    attended, d_query, d_key, d_value = lax.map(block_step, (to_blocks(queries), key_pairs, value_pairs, to_blocks(d_out), doc_blocks, key_docs, block_index))
    attended_all = attended.reshape(TOKENS, feature)
    group_width = HL * HD
    groups = feature // group_width
    branch = jnp.zeros((TOKENS, out_proj.shape[1]), jnp.float32)
    for group in range(groups):
        part = jnp.dot(attended_all[:, group * group_width:(group + 1) * group_width], out_proj[group * group_width:(group + 1) * group_width], preferred_element_type=jnp.float32).astype(jnp.bfloat16)
        part = lax.optimization_barrier(part)
        branch = branch + part.astype(jnp.float32)
    rebuilt = (stream.astype(jnp.float32) - branch).astype(jnp.bfloat16)
    zero_terms = jnp.zeros((1, TOK_DEV, head_count, HD), jnp.float32)
    key_total = d_key[:, TOK_DEV:] + jnp.concatenate([d_key[1:, :TOK_DEV], zero_terms], 0)
    value_total = d_value[:, TOK_DEV:] + jnp.concatenate([d_value[1:, :TOK_DEV], zero_terms], 0)
    grad_queries = d_query.reshape(TOKENS, feature)
    grad_keys = key_total.astype(jnp.bfloat16).reshape(TOKENS, feature)
    grad_values = value_total.astype(jnp.bfloat16).reshape(TOKENS, feature)
    return grad_queries, grad_keys, grad_values, rebuilt


def reference(queries, keys, values, stream, grad_stream, out_proj, doc_ids):
    results = []
    for section_index in range(SECTIONS):
        results.append(one_section(queries[section_index], keys[section_index], values[section_index], stream[section_index], grad_stream[section_index], out_proj[section_index], doc_ids[section_index]))
    grad_queries = jnp.stack([item[0] for item in results])
    grad_keys = jnp.stack([item[1] for item in results])
    grad_values = jnp.stack([item[2] for item in results])
    next_stream = jnp.stack([results[(section_index + 1) % SECTIONS][3] for section_index in range(SECTIONS)])
    next_grad = jnp.stack([grad_stream[(section_index + 1) % SECTIONS] for section_index in range(SECTIONS)])
    return (grad_queries, grad_keys, grad_values, next_stream, next_grad)
```

```python
import functools
import math

import jax
import jax.numpy as jnp
from jax import lax
from jax.experimental import pallas as pl
from jax.experimental.pallas import tpu as pltpu
from jax.sharding import PartitionSpec as P

HD = 128
WINDOW = 512
NEG = -1e30
MESH = pl.DeviceIdType.MESH
NT = (((1,), (1,)), ((), ()))
OWN, LEFT, RIGHT, FAR = 0, 1, 2, 3


def dot(a, b, dims=(((1,), (0,)), ((), ()))):
    return lax.dot_general(a, b, dims, preferred_element_type=jnp.float32)


def kernel(
    rows, width, shard, ctx_n, tp_n, pipe_n,
    q_hbm, k_hbm, v_hbm, s_hbm, g_hbm, w_hbm, doc_ref,
    dq_hbm, dk_hbm, dv_hbm, ns_hbm, ng_hbm,
    w_s, gat, q_s, k_s, v_s, st_s, acc, dot_s, att, bias,
    acck, accv, ret_out, ret_in, dq_s, fin, in_a, in_b, fin_l, fin_r,
    lsem, osem, ags, agr, fws, fwr, hs, hr, rts, rtr, rss, rsr, pgs, pgr, prs, prr,
):
    pipe = lax.axis_index("pipe")
    c = lax.axis_index("ctx")
    z = lax.axis_index("tp")
    right, left = lax.rem(z + 1, tp_n), lax.rem(z + tp_n - 1, tp_n)
    nxt, prv = lax.rem(c + 1, ctx_n), lax.rem(c + ctx_n - 1, ctx_n)
    other = lax.rem(pipe + 1, pipe_n)
    has_prev, has_next = c > 0, c < ctx_n - 1
    qb, sub, half = rows // 2, rows // 4, shard // 2
    kw = 3 * qb
    heads = width // HD

    barrier = pltpu.get_barrier_semaphore()
    for where in ({"tp": right}, {"tp": left}, {"ctx": nxt}, {"ctx": prv}, {"pipe": other}):
        pl.semaphore_signal(barrier, inc=1, device_id=where, device_id_type=MESH)

    def local(src, dst, sem):
        return pltpu.make_async_copy(src, dst, sem)

    shards = (z, left, right, lax.rem(z + 2, tp_n))
    loads = {}
    for rel in (OWN, LEFT, RIGHT, FAR):
        cols = pl.ds(pl.multiple_of(shards[rel] * shard, shard), shard)
        loads[rel] = local(w_hbm.at[0, :, cols], w_s.at[rel], lsem.at[rel])
    loads["g"] = local(g_hbm.at[0], gat.at[OWN], lsem.at[4])
    loads["q"] = local(q_hbm.at[0], q_s, lsem.at[5])
    loads["k"] = local(k_hbm.at[0], k_s.at[pl.ds(rows, rows)], lsem.at[6])
    loads["v"] = local(v_hbm.at[0], v_s.at[pl.ds(rows, rows)], lsem.at[7])
    loads["s"] = local(s_hbm.at[0], st_s, lsem.at[8])

    def remote(src, dst, ssem, rsem, where):
        return pltpu.make_async_remote_copy(
            src_ref=src, dst_ref=dst, send_sem=ssem, recv_sem=rsem,
            device_id=where, device_id_type=MESH,
        )

    to_right, to_left = {"tp": right}, {"tp": left}

    def piece(s):
        return pl.ds(s * sub, sub)

    lo, hi = pl.ds(0, half), pl.ds(half, half)

    def own(s):
        src = g_hbm.at[0, piece(s)]
        return (
            remote(src, gat.at[LEFT, piece(s)], ags.at[0, s], agr.at[0, s], to_right),
            remote(src, gat.at[RIGHT, piece(s)], ags.at[1, s], agr.at[1, s], to_left),
        )

    def passed(s):
        return (
            remote(gat.at[LEFT, piece(s), lo], gat.at[FAR, piece(s), lo], fws.at[0, s], fwr.at[0, s], to_right),
            remote(gat.at[RIGHT, piece(s), hi], gat.at[FAR, piece(s), hi], fws.at[1, s], fwr.at[1, s], to_left),
        )

    def halo():
        return (
            remote(k_hbm.at[0], k_s.at[pl.ds(0, rows)], hs.at[0], hr.at[0], {"ctx": nxt}),
            remote(v_hbm.at[0], v_s.at[pl.ds(0, rows)], hs.at[1], hr.at[1], {"ctx": nxt}),
        )

    def back(t):
        part = pl.ds(t * qb, qb)
        return tuple(
            remote(ret_out.at[i, part], ret_in.at[i, part], rts.at[i, t], rtr.at[i, t], {"ctx": prv})
            for i in range(2)
        )

    def far_terms(s):
        return (
            remote(gat.at[FAR, piece(s), lo], in_a.at[piece(s)], rss.at[0, 0, s], rsr.at[0, 0, s], to_right),
            remote(gat.at[FAR, piece(s), hi], in_b.at[piece(s)], rss.at[0, 1, s], rsr.at[0, 1, s], to_left),
        )

    def plain_terms(s):
        return (
            remote(gat.at[RIGHT, piece(s), hi], fin_l.at[piece(s), hi], rss.at[1, 0, s], rsr.at[1, 0, s], to_right),
            remote(gat.at[LEFT, piece(s), lo], fin_r.at[piece(s), lo], rss.at[1, 1, s], rsr.at[1, 1, s], to_left),
        )

    def merged_terms(s):
        return (
            remote(gat.at[RIGHT, piece(s), lo], fin_l.at[piece(s), lo], rss.at[2, 0, s], rsr.at[2, 0, s], to_right),
            remote(gat.at[LEFT, piece(s), hi], fin_r.at[piece(s), hi], rss.at[2, 1, s], rsr.at[2, 1, s], to_left),
        )

    def grad_on(s):
        return remote(g_hbm.at[0, piece(s)], ng_hbm.at[0, piece(s)], pgs.at[s], pgr.at[s], {"pipe": other})

    def stream_on(s):
        return remote(st_s.at[piece(s)], ns_hbm.at[0, piece(s)], prs.at[s], prr.at[s], {"pipe": other})

    def start(copies):
        for copy in copies:
            copy.start()

    def arrive(copies):
        for copy in copies:
            copy.wait_recv()

    def sent(copies):
        for copy in copies:
            copy.wait_send()

    loads["g"].start()
    for key in (OWN, "q", "k", "v", LEFT, RIGHT, FAR, "s"):
        loads[key].start()

    pl.semaphore_wait(barrier, 5)
    start(own(0))

    @pl.when(has_next)
    def _():
        start(halo())

    start(own(1))

    @pl.when(jnp.logical_not(has_prev))
    def _():
        k_s[pl.ds(0, rows), :] = jnp.zeros((rows, width), k_s.dtype)
        v_s[pl.ds(0, rows), :] = jnp.zeros((rows, width), v_s.dtype)

    @pl.when(jnp.logical_not(has_next))
    def _():
        ret_in[...] = jnp.zeros(ret_in.shape, ret_in.dtype)

    own_doc = doc_ref[:, pl.ds(pl.multiple_of(c * rows, rows), rows)].astype(jnp.float32)
    old_doc = doc_ref[:, pl.ds(pl.multiple_of(jnp.maximum(c - 1, 0) * rows, rows), rows)].astype(jnp.float32)
    key_row = jnp.concatenate([old_doc, own_doc], axis=1)
    key_doc = jnp.transpose(jnp.broadcast_to(key_row, (HD, 2 * rows)))
    a = lax.broadcasted_iota(jnp.int32, (kw, qb), 0)
    b = lax.broadcasted_iota(jnp.int32, (kw, qb), 1)
    for t in range(2):
        seen = (a <= b + rows) & (a > b + (rows - WINDOW))
        seen = seen & ((a + t * qb >= rows) | has_prev)
        columns = jnp.broadcast_to(key_doc[t * qb:t * qb + kw, :1], (kw, qb))
        seen = seen & (columns == own_doc[:, t * qb:(t + 1) * qb])
        bias[t] = jnp.where(seen, 0.0, NEG)

    kstep = min(512, shard)

    def d_out_term(t, rel, first):
        def step(i, _):
            cols = pl.ds(pl.multiple_of(i * kstep, kstep), kstep)
            term = dot(w_s[rel, :, cols], gat[rel, pl.ds(t * qb, qb), cols], NT)
            if first:
                @pl.when(i == 0)
                def _():
                    acc[...] = term

                @pl.when(i > 0)
                def _():
                    acc[...] += term
            else:
                acc[...] += term
            return 0

        lax.fori_loop(0, shard // kstep, step, 0)

    def d_out_store(t):
        dot_s[:, pl.ds(t * qb, qb)] = acc[...].astype(jnp.bfloat16)

    scaling = HD ** -0.5

    def head(h, t):
        cols = pl.ds(pl.multiple_of(h * HD, HD), HD)
        keys = k_s[pl.ds(t * qb, kw), cols]
        values = v_s[pl.ds(t * qb, kw), cols]
        queries = q_s[pl.ds(t * qb, qb), cols]
        d_out = dot_s[cols, pl.ds(t * qb, qb)]
        scores = dot(keys, queries, NT) + bias[t]
        top = jnp.max(scores, axis=0, keepdims=True)
        exponent = jnp.exp2((scores - top) * (scaling * math.log2(math.e)))
        total = jnp.sum(exponent, axis=0, keepdims=True)
        probs = exponent * (1.0 / total)
        weights = probs.astype(jnp.bfloat16)
        out = dot(jnp.transpose(values), weights)
        att[pl.ds(t * qb, qb), cols] = jnp.transpose(out).astype(jnp.bfloat16)
        out = out.astype(jnp.bfloat16).astype(jnp.float32)
        delta = jnp.sum(d_out.astype(jnp.float32) * out, axis=0, keepdims=True)
        d_prob = dot(values, d_out)
        d_score = (probs * (d_prob - delta)).astype(jnp.bfloat16)
        d_value = dot(weights, d_out, NT)
        d_key = dot(d_score, queries) * scaling
        d_query = dot(jnp.transpose(keys), d_score) * scaling
        dq_s[pl.ds(t * qb, qb), cols] = jnp.transpose(d_query).astype(jnp.bfloat16)
        for i, (total_ref, term) in enumerate(((acck, d_key), (accv, d_value))):
            if t == 0:
                ret_out[i, pl.ds(0, qb), cols] = term[:qb].astype(jnp.bfloat16)
                total_ref[pl.ds(0, 2 * qb), cols] = term[qb:]
            else:
                ret_out[i, pl.ds(qb, qb), cols] = (total_ref[pl.ds(0, qb), cols] + term[:qb]).astype(jnp.bfloat16)
                total_ref[pl.ds(qb, qb), cols] += term[qb:2 * qb]
                total_ref[pl.ds(2 * qb, qb), cols] = term[2 * qb:]

    def attention(t, hooks):
        def step(i, _):
            for at, hook in hooks.items():
                @pl.when(i == at)
                def _():
                    hook()
            for j in range(2):
                head(i * 2 + j, t)
            return 0

        lax.fori_loop(0, heads // 2, step, 0)

    nstep = min(512, shard)

    def partial(t, rel):
        def step(i, _):
            cols = pl.ds(pl.multiple_of(i * nstep, nstep), nstep)
            term = dot(att[pl.ds(t * qb, qb), :], w_s[rel, :, cols])
            gat[rel, pl.ds(t * qb, qb), cols] = term.astype(jnp.bfloat16)
            return 0

        lax.fori_loop(0, shard // nstep, step, 0)

    def pass_on(s):
        arrive(own(s))
        start(passed(s))

    def merge(s):
        arrive(far_terms(s))
        gat[RIGHT, piece(s), lo] = (
            gat[RIGHT, piece(s), lo].astype(jnp.float32) + in_a[piece(s), :].astype(jnp.float32)
        ).astype(jnp.bfloat16)
        gat[LEFT, piece(s), hi] = (
            gat[LEFT, piece(s), hi].astype(jnp.float32) + in_b[piece(s), :].astype(jnp.float32)
        ).astype(jnp.bfloat16)
        start(merged_terms(s))

    def finish(s):
        arrive(plain_terms(s))
        arrive(merged_terms(s))
        branch = (
            gat[OWN, piece(s), :].astype(jnp.float32)
            + fin_l[piece(s), :].astype(jnp.float32)
            + fin_r[piece(s), :].astype(jnp.float32)
        )
        st_s[piece(s), :] = (st_s[piece(s), :].astype(jnp.float32) - branch).astype(jnp.bfloat16)
        stream_on(s).start()

    loads[OWN].wait()
    loads["g"].wait()
    d_out_term(0, OWN, True)
    for key in (LEFT, RIGHT, FAR, "q", "k", "v"):
        loads[key].wait()
    pass_on(0)
    pass_on(1)
    start(own(2))
    start(own(3))
    d_out_term(0, LEFT, False)
    d_out_term(0, RIGHT, False)

    @pl.when(has_prev)
    def _():
        arrive(halo())

    for s in range(4):
        grad_on(s).start()
    arrive(passed(0))
    arrive(passed(1))
    d_out_term(0, FAR, False)
    d_out_store(0)

    last = heads // 2 - 1
    attention(0, {min(2, last): lambda: pass_on(2)})
    pass_on(3)

    @pl.when(has_prev)
    def _():
        start(back(0))

    out_q0 = local(dq_s.at[pl.ds(0, qb)], dq_hbm.at[0, pl.ds(0, qb)], osem.at[0])
    out_q0.start()
    sent(passed(0))
    sent(passed(1))
    partial(0, FAR)
    partial(0, RIGHT)
    start(far_terms(0))
    start(far_terms(1))
    partial(0, LEFT)
    start(plain_terms(0))
    start(plain_terms(1))
    partial(0, OWN)

    d_out_term(1, OWN, True)
    d_out_term(1, LEFT, False)
    d_out_term(1, RIGHT, False)
    arrive(passed(2))
    arrive(passed(3))
    d_out_term(1, FAR, False)
    d_out_store(1)
    attention(1, {min(2, last): lambda: merge(0), min(3, last): lambda: merge(1)} if last > 2 else {})
    if last <= 2:
        merge(0)
        merge(1)

    @pl.when(has_prev)
    def _():
        start(back(1))

    out_q1 = local(dq_s.at[pl.ds(qb, qb)], dq_hbm.at[0, pl.ds(qb, qb)], osem.at[1])
    out_q1.start()
    sent(passed(2))
    sent(passed(3))
    partial(1, FAR)
    partial(1, RIGHT)
    start(far_terms(2))
    start(far_terms(3))
    partial(1, LEFT)
    start(plain_terms(2))
    start(plain_terms(3))
    partial(1, OWN)
    loads["s"].wait()
    finish(0)
    finish(1)
    merge(2)
    merge(3)

    @pl.when(has_next)
    def _():
        arrive(back(0))
        arrive(back(1))

    outs = []
    for i, (total_ref, ref) in enumerate(((acck, dk_hbm), (accv, dv_hbm))):
        fin[i] = (total_ref[pl.ds(qb, rows), :] + ret_in[i].astype(jnp.float32)).astype(jnp.bfloat16)
        outs.append(local(fin.at[i], ref.at[0], osem.at[2 + i]))
        outs[-1].start()
    finish(2)
    finish(3)

    for s in range(4):
        sent(own(s))
        sent(far_terms(s))
        sent(plain_terms(s))
        sent(merged_terms(s))
        grad_on(s).wait_send()
        grad_on(s).wait_recv()
        stream_on(s).wait_send()
        stream_on(s).wait_recv()

    @pl.when(has_next)
    def _():
        sent(halo())

    @pl.when(has_prev)
    def _():
        sent(back(0))
        sent(back(1))

    for copy in (out_q0, out_q1, *outs):
        copy.wait()


def body(queries, keys, values, stream, grad_stream, out_proj, doc_ids):
    rows, width = queries.shape[1], queries.shape[2]
    shard = stream.shape[2]
    bf, f32 = jnp.bfloat16, jnp.float32
    qb = rows // 2
    dma = pltpu.SemaphoreType.DMA
    hbm = pl.BlockSpec(memory_space=pl.ANY)
    sizes = (lax.axis_size("ctx"), lax.axis_size("tp"), lax.axis_size("pipe"))
    assert sizes[1] == 4 and rows == WINDOW
    like = lambda x: jax.ShapeDtypeStruct(x.shape, x.dtype)
    return pl.pallas_call(
        functools.partial(kernel, rows, width, shard, *sizes),
        out_shape=(like(queries), like(keys), like(values), like(stream), like(grad_stream)),
        in_specs=[hbm] * 6 + [pl.BlockSpec(memory_space=pltpu.VMEM)],
        out_specs=(hbm,) * 5,
        scratch_shapes=[
            pltpu.VMEM((4, width, shard), bf),
            pltpu.VMEM((4, rows, shard), bf),
            pltpu.VMEM((rows, width), bf),
            pltpu.VMEM((2 * rows, width), bf),
            pltpu.VMEM((2 * rows, width), bf),
            pltpu.VMEM((rows, shard), bf),
            pltpu.VMEM((width, qb), f32),
            pltpu.VMEM((width, rows), bf),
            pltpu.VMEM((rows, width), bf),
            pltpu.VMEM((2, 3 * qb, qb), f32),
            pltpu.VMEM((3 * qb, width), f32),
            pltpu.VMEM((3 * qb, width), f32),
            pltpu.VMEM((2, rows, width), bf),
            pltpu.VMEM((2, rows, width), bf),
            pltpu.VMEM((rows, width), bf),
            pltpu.VMEM((2, rows, width), bf),
            pltpu.VMEM((rows, shard // 2), bf),
            pltpu.VMEM((rows, shard // 2), bf),
            pltpu.VMEM((rows, shard), bf),
            pltpu.VMEM((rows, shard), bf),
            dma((9,)), dma((4,)),
            dma((2, 4)), dma((2, 4)), dma((2, 4)), dma((2, 4)),
            dma((2,)), dma((2,)), dma((2, 2)), dma((2, 2)),
            dma((3, 2, 4)), dma((3, 2, 4)),
            dma((4,)), dma((4,)), dma((4,)), dma((4,)),
        ],
        compiler_params=pltpu.CompilerParams(
            collective_id=0, has_side_effects=True, vmem_limit_bytes=67043328
        ),
    )(queries, keys, values, stream, grad_stream, out_proj, doc_ids)


def solution(mesh):
    spec = P("pipe", "ctx", "tp")
    in_specs = (spec,) * 5 + (P("pipe", "tp", None), P("pipe", None))
    return jax.shard_map(body, mesh=mesh, in_specs=in_specs, out_specs=(spec,) * 5, check_vma=False)
```

```python
import functools
import math

import jax
import jax.numpy as jnp
from jax import lax
from jax.experimental import pallas as pl
from jax.experimental.pallas import tpu as pltpu
from jax.sharding import PartitionSpec as P

HD = 128
WINDOW = 512
NEG = -1e30
MESH = pl.DeviceIdType.MESH
NT = (((1,), (1,)), ((), ()))
OWN, RIGHT, FAR, LEFT = 0, 1, 2, 3
PAIRS = 4


def dot(a, b, dims=(((1,), (0,)), ((), ()))):
    return lax.dot_general(a, b, dims, preferred_element_type=jnp.float32)


def kernel(
    rows, width, shard, ctx_n, tp_n, pipe_n,
    q_hbm, k_hbm, v_hbm, s_hbm, g_hbm, w_hbm, doc_ref,
    dq_hbm, dk_hbm, dv_hbm, ns_hbm, ng_hbm,
    w_s, g_s, q_s, k_s, v_s, st_s, part, att, out_t, prob, bias,
    acc, ret_out, ret_in, mine, dq_s, in_a, in_b, fin_l, fin_r,
    lsem, osem, w1s, w1r, wxs, wxr, wcs, wcr, ats, atr, hs, hr, rts, rtr, rss, rsr, pgs, pgr, prs, prr,
):
    pipe = lax.axis_index("pipe")
    c = lax.axis_index("ctx")
    z = lax.axis_index("tp")
    nxt, prv = lax.rem(c + 1, ctx_n), lax.rem(c + ctx_n - 1, ctx_n)
    other = lax.rem(pipe + 1, pipe_n)
    has_prev, has_next = c > 0, c < ctx_n - 1
    qb, sub = rows // 2, rows // 4
    kw, pw = 3 * qb, 2 * HD
    row = c // 8
    x, core = lax.rem(c, 8) // 2, lax.rem(c, 2)
    mate = 1 - core
    xs = (x, lax.rem(x + 1, 4), lax.rem(x + 3, 4), lax.rem(x + 2, 4))

    def at_x(chip, side):
        return {"ctx": row * 8 + chip * 2 + side}

    to_z = {d: {"tp": lax.rem(z + d, tp_n)} for d in (RIGHT, FAR, LEFT)}
    x_up, x_down, x_mate = at_x(xs[1], core), at_x(xs[2], core), at_x(x, mate)

    barrier = pltpu.get_barrier_semaphore()
    partners = (*to_z.values(), x_up, x_down, x_mate, {"ctx": nxt}, {"ctx": prv}, {"pipe": other})
    for where in partners:
        pl.semaphore_signal(barrier, inc=1, device_id=where, device_id_type=MESH)

    def local(src, dst, sem):
        return pltpu.make_async_copy(src, dst, sem)

    def remote(src, dst, ssem, rsem, where):
        return pltpu.make_async_remote_copy(
            src_ref=src, dst_ref=dst, send_sem=ssem, recv_sem=rsem,
            device_id=where, device_id_type=MESH,
        )

    def features(d):
        return pl.ds(pl.multiple_of(lax.rem(z + d, tp_n) * shard, shard), shard)

    def block(chip, side):
        return pl.ds(pl.multiple_of((chip * 2 + side) * HD, HD), HD)

    def pair_rows(o):
        return pl.ds(pl.multiple_of(xs[o] * pw, pw), pw)

    loads = {
        "q": local(q_hbm.at[0], q_s, lsem.at[0]),
        "k": local(k_hbm.at[0], k_s.at[pl.ds(rows, rows)], lsem.at[1]),
        "v": local(v_hbm.at[0], v_s.at[pl.ds(rows, rows)], lsem.at[2]),
        "g": local(g_hbm.at[0], g_s, lsem.at[3]),
        "w": local(w_hbm.at[0, :, features(OWN)], w_s.at[OWN], lsem.at[4]),
        "s": local(s_hbm.at[0], st_s, lsem.at[5]),
    }

    def w_first(d):
        there = (4 - d) % 4
        here = block(x, core)
        return remote(w_hbm.at[0, here, features(d)], w_s.at[there, here], w1s.at[there - 1], w1r.at[there - 1], to_z[d])

    def w_piece(r, chip, side, ssem, rsem, where):
        here = w_s.at[r, block(chip, side)]
        return remote(here, here, ssem, rsem, where)

    def w_up(r, chip):
        return w_piece(r, chip, core, wxs.at[0, r - 1], wxr.at[0, r - 1], x_up)

    def w_down(r, chip):
        return w_piece(r, chip, core, wxs.at[1, r - 1], wxr.at[1, r - 1], x_down)

    def w_far(r, chip):
        return w_piece(r, chip, core, wxs.at[2, r - 1], wxr.at[2, r - 1], x_up if r == FAR else x_down)

    def w_mate(r, o, side):
        return w_piece(r, xs[o], side, wcs.at[o, r - 1], wcr.at[o, r - 1], x_mate)

    def own_block(r):
        w_first((4 - r) % 4).wait_recv()
        w_up(r, x).start()
        w_down(r, x).start()
        w_mate(r, 0, core).start()

    def up_block(r):
        w_down(r, xs[1]).wait_recv()
        if r != FAR:
            w_far(r, xs[1]).start()
        w_mate(r, 1, core).start()

    def down_block(r):
        w_up(r, xs[2]).wait_recv()
        if r == FAR:
            w_far(r, xs[2]).start()
        w_mate(r, 2, core).start()

    def far_block(r):
        w_far(r, xs[3]).wait_recv()
        w_mate(r, 3, core).start()

    def mate_blocks(o):
        for r in (LEFT, RIGHT, FAR):
            w_mate(r, o, mate).wait_recv()

    lo, hi = pl.ds(0, qb), pl.ds(qb, qb)

    def att_own(o):
        return (
            remote(att.at[OWN, o], att.at[LEFT, o], ats.at[0, o], atr.at[0, o], to_z[RIGHT]),
            remote(att.at[OWN, o], att.at[RIGHT, o], ats.at[1, o], atr.at[1, o], to_z[LEFT]),
        )

    def att_pass(o):
        return (
            remote(att.at[LEFT, o, lo], att.at[FAR, o, lo], ats.at[2, o], atr.at[2, o], to_z[RIGHT]),
            remote(att.at[RIGHT, o, hi], att.at[FAR, o, hi], ats.at[3, o], atr.at[3, o], to_z[LEFT]),
        )

    def far_terms(o):
        return (
            remote(part.at[o, FAR, :, lo], in_a.at[o], rss.at[0, 0, o], rsr.at[0, 0, o], to_z[RIGHT]),
            remote(part.at[o, FAR, :, hi], in_b.at[o], rss.at[0, 1, o], rsr.at[0, 1, o], to_z[LEFT]),
        )

    def plain_terms(o):
        return (
            remote(part.at[o, RIGHT, :, hi], fin_l.at[o, :, hi], rss.at[1, 0, o], rsr.at[1, 0, o], to_z[RIGHT]),
            remote(part.at[o, LEFT, :, lo], fin_r.at[o, :, lo], rss.at[1, 1, o], rsr.at[1, 1, o], to_z[LEFT]),
        )

    def merged_terms(o):
        return (
            remote(part.at[o, RIGHT, :, lo], fin_l.at[o, :, lo], rss.at[2, 0, o], rsr.at[2, 0, o], to_z[RIGHT]),
            remote(part.at[o, LEFT, :, hi], fin_r.at[o, :, hi], rss.at[2, 1, o], rsr.at[2, 1, o], to_z[LEFT]),
        )

    def halo():
        return (
            remote(k_hbm.at[0], k_s.at[pl.ds(0, rows)], hs.at[0], hr.at[0], {"ctx": nxt}),
            remote(v_hbm.at[0], v_s.at[pl.ds(0, rows)], hs.at[1], hr.at[1], {"ctx": nxt}),
        )

    def back(p):
        return tuple(
            remote(ret_out.at[i, p], ret_in.at[i, p], rts.at[i, p], rtr.at[i, p], {"ctx": prv})
            for i in range(2)
        )

    def grad_on(s):
        here = pl.ds(s * sub, sub)
        return remote(g_hbm.at[0, here], ng_hbm.at[0, here], pgs.at[s], pgr.at[s], {"pipe": other})

    wide = shard // 4

    def stream_on(n):
        cols = pl.ds(n * wide, wide)
        return remote(st_s.at[:, cols], ns_hbm.at[0, :, cols], prs.at[n], prr.at[n], {"pipe": other})

    def start(copies):
        for copy in copies:
            copy.start()

    def arrive(copies):
        for copy in copies:
            copy.wait_recv()

    def sent(copies):
        for copy in copies:
            copy.wait_send()

    def fill_bias():
        own_doc = doc_ref[:, pl.ds(pl.multiple_of(c * rows, rows), rows)].astype(jnp.float32)
        old_doc = doc_ref[:, pl.ds(pl.multiple_of(jnp.maximum(c - 1, 0) * rows, rows), rows)].astype(jnp.float32)
        key_doc = jnp.transpose(jnp.broadcast_to(jnp.concatenate([old_doc, own_doc], axis=1), (HD, 2 * rows)))
        a = lax.broadcasted_iota(jnp.int32, (kw, qb), 0)
        b = lax.broadcasted_iota(jnp.int32, (kw, qb), 1)
        for t in range(2):
            seen = (a <= b + rows) & (a > b + (rows - WINDOW))
            seen = seen & ((a + t * qb >= rows) | has_prev)
            columns = jnp.broadcast_to(key_doc[t * qb:t * qb + kw, :1], (kw, qb))
            seen = seen & (columns == own_doc[:, t * qb:(t + 1) * qb])
            bias[t] = jnp.where(seen, 0.0, NEG)

    scaling = HD ** -0.5

    def forward(o):
        def step(i, _):
            cols = pl.ds(pl.multiple_of(xs[o] * pw + i * HD, HD), HD)
            mine_cols = pl.ds(pl.multiple_of(i * HD, HD), HD)
            for t in range(2):
                tokens = pl.ds(t * qb, qb)
                keys = k_s[pl.ds(t * qb, kw), cols]
                values = v_s[pl.ds(t * qb, kw), cols]
                scores = dot(keys, q_s[tokens, cols], NT) + bias[t]
                top = jnp.max(scores, axis=0, keepdims=True)
                exponent = jnp.exp2((scores - top) * (scaling * math.log2(math.e)))
                total = jnp.sum(exponent, axis=0, keepdims=True)
                weights = (exponent * (1.0 / total)).astype(jnp.bfloat16)
                prob[o * 2 + i, t] = weights
                out = dot(jnp.transpose(values), weights)
                out_t[o, mine_cols, tokens] = out.astype(jnp.bfloat16)
                att[OWN, o, tokens, mine_cols] = jnp.transpose(out).astype(jnp.bfloat16)
            return 0

        lax.fori_loop(0, 2, step, 0)

    def d_out_terms(o):
        def step(r, _):
            term = dot(w_s[r, pair_rows(o), :], g_s[...], NT)
            part[o, r] = term.astype(jnp.bfloat16)
            return 0

        lax.fori_loop(0, 4, step, 0)

    def add_into(r, o, cols, extra):
        part[o, r, :, cols] = (
            part[o, r, :, cols].astype(jnp.float32) + extra.astype(jnp.float32)
        ).astype(jnp.bfloat16)

    def merge(o):
        arrive(far_terms(o))
        add_into(RIGHT, o, lo, in_a[o])
        add_into(LEFT, o, hi, in_b[o])
        start(merged_terms(o))

    def d_out_done(o):
        arrive(plain_terms(o))
        arrive(merged_terms(o))
        total = part[o, OWN].astype(jnp.float32) + fin_l[o].astype(jnp.float32) + fin_r[o].astype(jnp.float32)
        part[o, OWN] = total.astype(jnp.bfloat16)

    def backward(o):
        def step(i, _):
            cols = pl.ds(pl.multiple_of(xs[o] * pw + i * HD, HD), HD)
            mine_cols = pl.ds(pl.multiple_of(i * HD, HD), HD)
            d_keys, d_values = [], []
            for t in range(2):
                tokens = pl.ds(t * qb, qb)
                keys = k_s[pl.ds(t * qb, kw), cols]
                values = v_s[pl.ds(t * qb, kw), cols]
                queries = q_s[tokens, cols]
                d_out = part[o, OWN, mine_cols, tokens]
                weights = prob[o * 2 + i, t]
                delta = jnp.sum(
                    d_out.astype(jnp.float32) * out_t[o, mine_cols, tokens].astype(jnp.float32),
                    axis=0, keepdims=True,
                )
                d_prob = dot(values, d_out)
                d_score = (weights.astype(jnp.float32) * (d_prob - delta)).astype(jnp.bfloat16)
                d_values.append(dot(weights, d_out, NT))
                d_keys.append(dot(d_score, queries) * scaling)
                d_query = dot(jnp.transpose(keys), d_score) * scaling
                dq_s[tokens, cols] = jnp.transpose(d_query).astype(jnp.bfloat16)
            for n, (early, late) in enumerate((d_keys, d_values)):
                ret_out[n, xs[o], pl.ds(0, qb), mine_cols] = early[:qb].astype(jnp.bfloat16)
                ret_out[n, xs[o], pl.ds(qb, qb), mine_cols] = (early[qb:2 * qb] + late[:qb]).astype(jnp.bfloat16)
                mine[n, o, pl.ds(0, qb), mine_cols] = early[2 * qb:] + late[qb:2 * qb]
                mine[n, o, pl.ds(qb, qb), mine_cols] = late[2 * qb:]
            return 0

        lax.fori_loop(0, 2, step, 0)

        @pl.when(has_prev)
        def _():
            start(back(xs[o]))

    def branch_term(o, cols):
        left = jnp.concatenate([att[r, o] for r in range(4)], axis=1)
        return dot(left, w_s[:, pair_rows(o), cols].reshape(4 * pw, wide))

    def branch(o):
        def step(n, _):
            cols = pl.ds(pl.multiple_of(n * wide, wide), wide)
            term = branch_term(o, cols)
            acc[:, cols] = term if o == 0 else acc[:, cols] + term
            return 0

        lax.fori_loop(0, 4, step, 0)

    def rebuild(n):
        cols = pl.ds(n * wide, wide)
        total = acc[:, cols] + branch_term(3, cols)
        st_s[:, cols] = (st_s[:, cols].astype(jnp.float32) - total).astype(jnp.bfloat16)

    def att_relay(o):
        arrive(att_own(o))
        start(att_pass(o))

    for key in ("k", "v", "q", "w", "g", "s"):
        loads[key].start()

    pl.semaphore_wait(barrier, len(partners))
    w_first(RIGHT).start()
    w_first(LEFT).start()

    @pl.when(has_next)
    def _():
        start(halo())

    w_first(FAR).start()

    @pl.when(jnp.logical_not(has_prev))
    def _():
        k_s[pl.ds(0, rows), :] = jnp.zeros((rows, width), k_s.dtype)
        v_s[pl.ds(0, rows), :] = jnp.zeros((rows, width), v_s.dtype)

    @pl.when(jnp.logical_not(has_next))
    def _():
        ret_in[...] = jnp.zeros(ret_in.shape, ret_in.dtype)

    fill_bias()
    for key in ("k", "v", "q"):
        loads[key].wait()
    own_block(LEFT)
    own_block(RIGHT)
    own_block(FAR)

    @pl.when(has_prev)
    def _():
        arrive(halo())

    for s in range(4):
        grad_on(s).start()
    forward(0)
    start(att_own(0))
    up_block(LEFT)
    loads["w"].wait()
    loads["g"].wait()
    mate_blocks(0)
    d_out_terms(0)
    start(far_terms(0))
    start(plain_terms(0))
    forward(1)
    start(att_own(1))
    att_relay(0)
    merge(0)
    up_block(RIGHT)
    down_block(LEFT)
    forward(2)
    start(att_own(2))
    att_relay(1)
    forward(3)
    start(att_own(3))
    att_relay(2)
    d_out_done(0)
    down_block(RIGHT)
    up_block(FAR)
    arrive(att_pass(0))
    branch(0)
    att_relay(3)
    mate_blocks(1)
    d_out_terms(1)
    start(far_terms(1))
    start(plain_terms(1))
    backward(0)
    merge(1)
    far_block(LEFT)
    down_block(FAR)
    arrive(att_pass(1))
    branch(1)
    mate_blocks(2)
    d_out_terms(2)
    start(far_terms(2))
    start(plain_terms(2))
    arrive(att_pass(2))
    branch(2)
    far_block(RIGHT)
    far_block(FAR)
    arrive(att_pass(3))
    loads["s"].wait()
    mate_blocks(3)
    for n in range(4):
        rebuild(n)
        stream_on(n).start()
    d_out_terms(3)
    start(far_terms(3))
    start(plain_terms(3))
    merge(2)
    d_out_done(1)
    backward(1)
    merge(3)
    d_out_done(2)
    backward(2)
    d_out_done(3)
    backward(3)

    out_q = local(dq_s, dq_hbm.at[0], osem.at[0])
    out_q.start()
    outs = [out_q]

    @pl.when(has_next)
    def _():
        for p in range(PAIRS):
            arrive(back(p))

    for i, (ref, out) in enumerate(((k_s, dk_hbm), (v_s, dv_hbm))):
        here = ref.at[pl.ds(rows, rows)]
        for o in range(PAIRS):
            total = mine[i, o] + ret_in[i, xs[o]].astype(jnp.float32)
            ref[pl.ds(rows, rows), pair_rows(o)] = total.astype(jnp.bfloat16)
        outs.append(local(here, out.at[0], osem.at[1 + i]))
        outs[-1].start()

    for r in (LEFT, RIGHT, FAR):
        w_first((4 - r) % 4).wait_send()
        w_up(r, x).wait_send()
        w_down(r, x).wait_send()
        w_far(r, xs[1] if r != FAR else xs[2]).wait_send()
        for o in range(PAIRS):
            w_mate(r, o, core).wait_send()
    for o in range(PAIRS):
        sent(att_own(o))
        sent(att_pass(o))
        sent(far_terms(o))
        sent(plain_terms(o))
        sent(merged_terms(o))
        grad_on(o).wait_send()
        grad_on(o).wait_recv()
        stream_on(o).wait_send()
        stream_on(o).wait_recv()

    @pl.when(has_next)
    def _():
        sent(halo())

    @pl.when(has_prev)
    def _():
        for p in range(PAIRS):
            sent(back(p))

    for copy in outs:
        copy.wait()


def body(queries, keys, values, stream, grad_stream, out_proj, doc_ids):
    rows, width = queries.shape[1], queries.shape[2]
    shard = stream.shape[2]
    bf, f32 = jnp.bfloat16, jnp.float32
    qb, pw = rows // 2, 2 * HD
    dma = pltpu.SemaphoreType.DMA
    hbm = pl.BlockSpec(memory_space=pl.ANY)
    sizes = (lax.axis_size("ctx"), lax.axis_size("tp"), lax.axis_size("pipe"))
    assert sizes[0] % 8 == 0 and sizes[1] == 4 and rows == WINDOW and width == 8 * HD
    like = lambda x: jax.ShapeDtypeStruct(x.shape, x.dtype)
    return pl.pallas_call(
        functools.partial(kernel, rows, width, shard, *sizes),
        out_shape=(like(queries), like(keys), like(values), like(stream), like(grad_stream)),
        in_specs=[hbm] * 6 + [pl.BlockSpec(memory_space=pltpu.VMEM)],
        out_specs=(hbm,) * 5,
        scratch_shapes=[
            pltpu.VMEM((4, width, shard), bf),
            pltpu.VMEM((rows, shard), bf),
            pltpu.VMEM((rows, width), bf),
            pltpu.VMEM((2 * rows, width), bf),
            pltpu.VMEM((2 * rows, width), bf),
            pltpu.VMEM((rows, shard), bf),
            pltpu.VMEM((PAIRS, 4, pw, rows), bf),
            pltpu.VMEM((4, PAIRS, rows, pw), bf),
            pltpu.VMEM((PAIRS, pw, rows), bf),
            pltpu.VMEM((8, 2, 3 * qb, qb), bf),
            pltpu.VMEM((2, 3 * qb, qb), f32),
            pltpu.VMEM((rows, shard), f32),
            pltpu.VMEM((2, PAIRS, rows, pw), bf),
            pltpu.VMEM((2, PAIRS, rows, pw), bf),
            pltpu.VMEM((2, PAIRS, rows, pw), f32),
            pltpu.VMEM((rows, width), bf),
            pltpu.VMEM((PAIRS, pw, qb), bf),
            pltpu.VMEM((PAIRS, pw, qb), bf),
            pltpu.VMEM((PAIRS, pw, rows), bf),
            pltpu.VMEM((PAIRS, pw, rows), bf),
            dma((6,)), dma((3,)),
            dma((3,)), dma((3,)), dma((3, 3)), dma((3, 3)), dma((4, 3)), dma((4, 3)),
            dma((4, 4)), dma((4, 4)),
            dma((2,)), dma((2,)), dma((2, 4)), dma((2, 4)),
            dma((3, 2, 4)), dma((3, 2, 4)),
            dma((4,)), dma((4,)), dma((4,)), dma((4,)),
        ],
        compiler_params=pltpu.CompilerParams(
            collective_id=0, has_side_effects=True, vmem_limit_bytes=67043328
        ),
    )(queries, keys, values, stream, grad_stream, out_proj, doc_ids)


def solution(mesh):
    spec = P("pipe", "ctx", "tp")
    in_specs = (spec,) * 5 + (P("pipe", "tp", None), P("pipe", None))
    return jax.shard_map(body, mesh=mesh, in_specs=in_specs, out_specs=(spec,) * 5, check_vma=False)
```

```python
import functools
import math

import jax
import jax.numpy as jnp
from jax import lax
from jax.experimental import pallas as pl
from jax.experimental.pallas import tpu as pltpu
from jax.sharding import PartitionSpec as P

HD = 128
WINDOW = 512
NEG = -1e30
MESH = pl.DeviceIdType.MESH
NT = (((1,), (1,)), ((), ()))
OWN, RIGHT, FAR, LEFT = 0, 1, 2, 3
PAIRS = 4


def dot(a, b, dims=(((1,), (0,)), ((), ()))):
    return lax.dot_general(a, b, dims, preferred_element_type=jnp.float32)


def kernel(
    rows, width, shard, ctx_n, tp_n, pipe_n,
    q_hbm, k_hbm, v_hbm, s_hbm, g_hbm, w_hbm, doc_ref,
    dq_hbm, dk_hbm, dv_hbm, ns_hbm, ng_hbm,
    w_s, g_s, q_s, k_s, v_s, st_s, part, att, out_t, prob, bias,
    acc, ret_out, ret_in, relay, mine, dq_s, in_a, in_b, fin_l, fin_r,
    lsem, osem, w1s, w1r, wxs, wxr, wcs, wcr, ats, atr, hs, hr, rts, rtr, rls, rlr, rss, rsr, pgs, pgr, prs, prr,
):
    pipe = lax.axis_index("pipe")
    c = lax.axis_index("ctx")
    z = lax.axis_index("tp")
    nxt, prv = lax.rem(c + 1, ctx_n), lax.rem(c + ctx_n - 1, ctx_n)
    other = lax.rem(pipe + 1, pipe_n)
    has_prev, has_next = c > 0, c < ctx_n - 1
    qb, sub = rows // 2, rows // 4
    kw, pw = 3 * qb, 2 * HD
    row = c // 8
    x, core = lax.rem(c, 8) // 2, lax.rem(c, 2)
    mate = 1 - core
    xs = (x, lax.rem(x + 1, 4), lax.rem(x + 3, 4), lax.rem(x + 2, 4))

    def at_x(chip, side):
        return {"ctx": row * 8 + chip * 2 + side}

    to_z = {d: {"tp": lax.rem(z + d, tp_n)} for d in (RIGHT, FAR, LEFT)}
    x_up, x_down, x_mate = at_x(xs[1], core), at_x(xs[2], core), at_x(x, mate)

    barrier = pltpu.get_barrier_semaphore()
    partners = (*to_z.values(), x_up, x_down, x_mate, {"ctx": nxt}, {"ctx": prv}, {"pipe": other})
    for where in partners:
        pl.semaphore_signal(barrier, inc=1, device_id=where, device_id_type=MESH)

    more_rows = c < ctx_n - 8
    is_first = (lax.rem(c, 8) == 0) & has_prev
    is_relay = (core == 0) & (x < 3) & more_rows
    is_last = (lax.rem(c, 8) == 7) & more_rows
    row_last = {"ctx": row * 8 + 7}
    row_next = {"ctx": lax.rem(row * 8 + 8, ctx_n)}

    @pl.when(is_relay)
    def _():
        pl.semaphore_signal(barrier, inc=1, device_id=row_next, device_id_type=MESH)

    @pl.when(is_last)
    def _():
        for chip in range(3):
            pl.semaphore_signal(barrier, inc=1, device_id=at_x(chip, 0), device_id_type=MESH)

    def local(src, dst, sem):
        return pltpu.make_async_copy(src, dst, sem)

    def remote(src, dst, ssem, rsem, where):
        return pltpu.make_async_remote_copy(
            src_ref=src, dst_ref=dst, send_sem=ssem, recv_sem=rsem,
            device_id=where, device_id_type=MESH,
        )

    def features(d):
        return pl.ds(pl.multiple_of(lax.rem(z + d, tp_n) * shard, shard), shard)

    def block(chip, side):
        return pl.ds(pl.multiple_of((chip * 2 + side) * HD, HD), HD)

    def pair_rows(o):
        return pl.ds(pl.multiple_of(xs[o] * pw, pw), pw)

    loads = {
        "q": local(q_hbm.at[0], q_s, lsem.at[0]),
        "k": local(k_hbm.at[0], k_s.at[pl.ds(rows, rows)], lsem.at[1]),
        "v": local(v_hbm.at[0], v_s.at[pl.ds(rows, rows)], lsem.at[2]),
        "g": local(g_hbm.at[0], g_s, lsem.at[3]),
        "w": local(w_hbm.at[0, :, features(OWN)], w_s.at[OWN], lsem.at[4]),
        "s": local(s_hbm.at[0], st_s, lsem.at[5]),
    }

    part_f = shard // 2

    def w_first(d, f):
        there = (4 - d) % 4
        here = block(x, core)
        start_at = lax.rem(z + d, tp_n) * shard + f * part_f
        cols = pl.ds(pl.multiple_of(start_at, part_f), part_f)
        return remote(
            w_hbm.at[0, here, cols], w_s.at[there, here, pl.ds(f * part_f, part_f)],
            w1s.at[there - 1, f], w1r.at[there - 1, f], to_z[d],
        )

    def w_piece(r, f, chip, side, ssem, rsem, where):
        here = w_s.at[r, block(chip, side), pl.ds(f * part_f, part_f)]
        return remote(here, here, ssem, rsem, where)

    def w_up(r, f, chip):
        return w_piece(r, f, chip, core, wxs.at[0, r - 1, f], wxr.at[0, r - 1, f], x_up)

    def w_down(r, f, chip):
        return w_piece(r, f, chip, core, wxs.at[1, r - 1, f], wxr.at[1, r - 1, f], x_down)

    upward = ((RIGHT, 1), (FAR, 1))

    def w_far(r, f, chip):
        where = x_up if (r, f) in upward else x_down
        return w_piece(r, f, chip, core, wxs.at[2, r - 1, f], wxr.at[2, r - 1, f], where)

    def w_mate(r, f, o, side):
        return w_piece(r, f, xs[o], side, wcs.at[o, r - 1, f], wcr.at[o, r - 1, f], x_mate)

    def own_block(r, f):
        w_first((4 - r) % 4, f).wait_recv()
        w_up(r, f, x).start()
        w_down(r, f, x).start()
        w_mate(r, f, 0, core).start()

    def up_block(r, f):
        w_down(r, f, xs[1]).wait_recv()
        if (r, f) not in upward:
            w_far(r, f, xs[1]).start()
        w_mate(r, f, 1, core).start()

    def down_block(r, f):
        w_up(r, f, xs[2]).wait_recv()
        if (r, f) in upward:
            w_far(r, f, xs[2]).start()
        w_mate(r, f, 2, core).start()

    def far_block(r, f):
        w_far(r, f, xs[3]).wait_recv()
        w_mate(r, f, 3, core).start()

    def mate_blocks(o, halves=(0, 1)):
        for f in halves:
            for r in (LEFT, RIGHT, FAR):
                w_mate(r, f, o, mate).wait_recv()

    lo, hi = pl.ds(0, qb), pl.ds(qb, qb)

    def att_own(o):
        return (
            remote(att.at[OWN, o], att.at[LEFT, o], ats.at[0, o], atr.at[0, o], to_z[RIGHT]),
            remote(att.at[OWN, o], att.at[RIGHT, o], ats.at[1, o], atr.at[1, o], to_z[LEFT]),
        )

    def att_pass(o):
        return (
            remote(att.at[LEFT, o, lo], att.at[FAR, o, lo], ats.at[2, o], atr.at[2, o], to_z[RIGHT]),
            remote(att.at[RIGHT, o, hi], att.at[FAR, o, hi], ats.at[3, o], atr.at[3, o], to_z[LEFT]),
        )

    def far_terms(o):
        return (
            remote(part.at[o, FAR, :, lo], in_a.at[o], rss.at[0, 0, o], rsr.at[0, 0, o], to_z[RIGHT]),
            remote(part.at[o, FAR, :, hi], in_b.at[o], rss.at[0, 1, o], rsr.at[0, 1, o], to_z[LEFT]),
        )

    def plain_terms(o):
        return (
            remote(part.at[o, RIGHT, :, hi], fin_l.at[o, :, hi], rss.at[1, 0, o], rsr.at[1, 0, o], to_z[RIGHT]),
            remote(part.at[o, LEFT, :, lo], fin_r.at[o, :, lo], rss.at[1, 1, o], rsr.at[1, 1, o], to_z[LEFT]),
        )

    def merged_terms(o):
        return (
            remote(part.at[o, RIGHT, :, lo], fin_l.at[o, :, lo], rss.at[2, 0, o], rsr.at[2, 0, o], to_z[RIGHT]),
            remote(part.at[o, LEFT, :, hi], fin_r.at[o, :, hi], rss.at[2, 1, o], rsr.at[2, 1, o], to_z[LEFT]),
        )

    def halo():
        return (
            remote(k_hbm.at[0], k_s.at[pl.ds(0, rows)], hs.at[0], hr.at[0], {"ctx": nxt}),
            remote(v_hbm.at[0], v_s.at[pl.ds(0, rows)], hs.at[1], hr.at[1], {"ctx": nxt}),
        )

    def back(p):
        return tuple(
            remote(ret_out.at[i, p], ret_in.at[i, p], rts.at[i, p], rtr.at[i, p], {"ctx": prv})
            for i in range(2)
        )

    def to_relay(o):
        where = {"ctx": jnp.maximum(row - 1, 0) * 8 + o * 2}
        return tuple(
            remote(ret_out.at[i, xs[o]], relay.at[i], rls.at[i, o], rlr.at[i], where)
            for i in range(2)
        )

    def from_relay():
        p = x + x // 2
        return tuple(
            remote(relay.at[i], ret_in.at[i, p], rts.at[i, 4], rtr.at[i, p], row_last)
            for i in range(2)
        )

    def relay_on(chip):
        @pl.when(is_relay & (x == chip))
        def _():
            arrive(tuple(
                remote(ret_out.at[i, 0], relay.at[i], rls.at[i, 0], rlr.at[i], row_next) for i in range(2)
            ))
            start(from_relay())

    def grad_on(s):
        here = pl.ds(s * sub, sub)
        return remote(g_hbm.at[0, here], ng_hbm.at[0, here], pgs.at[s], pgr.at[s], {"pipe": other})

    wide = shard // 4

    def stream_on(n):
        cols = pl.ds(n * wide, wide)
        return remote(st_s.at[:, cols], ns_hbm.at[0, :, cols], prs.at[n], prr.at[n], {"pipe": other})

    def start(copies):
        for copy in copies:
            copy.start()

    def arrive(copies):
        for copy in copies:
            copy.wait_recv()

    def sent(copies):
        for copy in copies:
            copy.wait_send()

    def fill_bias():
        own_doc = doc_ref[:, pl.ds(pl.multiple_of(c * rows, rows), rows)].astype(jnp.float32)
        old_doc = doc_ref[:, pl.ds(pl.multiple_of(jnp.maximum(c - 1, 0) * rows, rows), rows)].astype(jnp.float32)
        key_doc = jnp.transpose(jnp.broadcast_to(jnp.concatenate([old_doc, own_doc], axis=1), (HD, 2 * rows)))
        a = lax.broadcasted_iota(jnp.int32, (kw, qb), 0)
        b = lax.broadcasted_iota(jnp.int32, (kw, qb), 1)
        for t in range(2):
            seen = (a <= b + rows) & (a > b + (rows - WINDOW))
            seen = seen & ((a + t * qb >= rows) | has_prev)
            columns = jnp.broadcast_to(key_doc[t * qb:t * qb + kw, :1], (kw, qb))
            seen = seen & (columns == own_doc[:, t * qb:(t + 1) * qb])
            bias[t] = jnp.where(seen, 0.0, NEG)

    scaling = HD ** -0.5

    def forward(o):
        def step(i, _):
            cols = pl.ds(pl.multiple_of(xs[o] * pw + i * HD, HD), HD)
            mine_cols = pl.ds(pl.multiple_of(i * HD, HD), HD)
            for t in range(2):
                tokens = pl.ds(t * qb, qb)
                keys = k_s[pl.ds(t * qb, kw), cols]
                values = v_s[pl.ds(t * qb, kw), cols]
                scores = dot(keys, q_s[tokens, cols], NT) + bias[t]
                top = jnp.max(scores, axis=0, keepdims=True)
                exponent = jnp.exp2((scores - top) * (scaling * math.log2(math.e)))
                total = jnp.sum(exponent, axis=0, keepdims=True)
                weights = (exponent * (1.0 / total)).astype(jnp.bfloat16)
                prob[o * 2 + i, t] = weights
                out = dot(jnp.transpose(values), weights)
                out_t[o, mine_cols, tokens] = out.astype(jnp.bfloat16)
                att[OWN, o, tokens, mine_cols] = jnp.transpose(out).astype(jnp.bfloat16)
            return 0

        lax.fori_loop(0, 2, step, 0)

    def d_out_terms(o):
        def step(r, _):
            term = dot(w_s[r, pair_rows(o), :], g_s[...], NT)
            part[o, r] = term.astype(jnp.bfloat16)
            return 0

        lax.fori_loop(0, 4, step, 0)

    def add_into(r, o, cols, extra):
        part[o, r, :, cols] = (
            part[o, r, :, cols].astype(jnp.float32) + extra.astype(jnp.float32)
        ).astype(jnp.bfloat16)

    def merge(o):
        arrive(far_terms(o))
        add_into(RIGHT, o, lo, in_a[o])
        add_into(LEFT, o, hi, in_b[o])
        start(merged_terms(o))

    def d_out_done(o):
        arrive(plain_terms(o))
        arrive(merged_terms(o))
        total = part[o, OWN].astype(jnp.float32) + fin_l[o].astype(jnp.float32) + fin_r[o].astype(jnp.float32)
        part[o, OWN] = total.astype(jnp.bfloat16)

    def backward(o):
        def step(i, _):
            cols = pl.ds(pl.multiple_of(xs[o] * pw + i * HD, HD), HD)
            mine_cols = pl.ds(pl.multiple_of(i * HD, HD), HD)
            d_keys, d_values = [], []
            for t in range(2):
                tokens = pl.ds(t * qb, qb)
                keys = k_s[pl.ds(t * qb, kw), cols]
                values = v_s[pl.ds(t * qb, kw), cols]
                queries = q_s[tokens, cols]
                d_out = part[o, OWN, mine_cols, tokens]
                weights = prob[o * 2 + i, t]
                delta = jnp.sum(
                    d_out.astype(jnp.float32) * out_t[o, mine_cols, tokens].astype(jnp.float32),
                    axis=0, keepdims=True,
                )
                d_prob = dot(values, d_out)
                d_score = (weights.astype(jnp.float32) * (d_prob - delta)).astype(jnp.bfloat16)
                d_values.append(dot(weights, d_out, NT))
                d_keys.append(dot(d_score, queries) * scaling)
                d_query = dot(jnp.transpose(keys), d_score) * scaling
                dq_s[tokens, cols] = jnp.transpose(d_query).astype(jnp.bfloat16)
            for n, (early, late) in enumerate((d_keys, d_values)):
                ret_out[n, xs[o], pl.ds(0, qb), mine_cols] = early[:qb].astype(jnp.bfloat16)
                ret_out[n, xs[o], pl.ds(qb, qb), mine_cols] = (early[qb:2 * qb] + late[:qb]).astype(jnp.bfloat16)
                mine[n, xs[o], pl.ds(0, qb), mine_cols] = early[2 * qb:] + late[qb:2 * qb]
                mine[n, xs[o], pl.ds(qb, qb), mine_cols] = late[2 * qb:]
            return 0

        lax.fori_loop(0, 2, step, 0)

        @pl.when(has_prev if o == 3 else has_prev & jnp.logical_not(is_first))
        def _():
            start(back(xs[o]))

        if o < 3:
            @pl.when(is_first)
            def _():
                start(to_relay(o))

        local(dq_s.at[:, pair_rows(o)], dq_hbm.at[0, :, pair_rows(o)], osem.at[0, o]).start()

    def rebuild(n):
        cols = pl.ds(n * wide, wide)

        def step(o, _):
            pair = lax.rem(x + o + o // 2 - 2 * (o // 3), 4)
            heads = pl.ds(pl.multiple_of(pair * pw, pw), pw)
            left = jnp.concatenate([att[r, o] for r in range(4)], axis=1)
            term = dot(left, w_s[:, heads, cols].reshape(4 * pw, wide))

            @pl.when(o == 0)
            def _():
                acc[...] = term

            @pl.when(o > 0)
            def _():
                acc[...] += term

            return 0

        lax.fori_loop(0, PAIRS, step, 0)
        st_s[:, cols] = (st_s[:, cols].astype(jnp.float32) - acc[...]).astype(jnp.bfloat16)
        stream_on(n).start()

    def att_relay(o):
        arrive(att_own(o))
        start(att_pass(o))

    for key in ("k", "v", "q", "w", "g", "s"):
        loads[key].start()

    awaited = len(partners) + jnp.where(is_first, 3, 0) + jnp.where(is_relay, 1, 0)
    pl.semaphore_wait(barrier, awaited)
    for f in range(2):
        w_first(RIGHT, f).start()
        w_first(LEFT, f).start()

    @pl.when(has_next)
    def _():
        start(halo())

    for f in range(2):
        w_first(FAR, f).start()

    @pl.when(x > 0)
    def _():
        for s in range(4):
            grad_on(s).start()

    @pl.when(jnp.logical_not(has_prev))
    def _():
        k_s[pl.ds(0, rows), :] = jnp.zeros((rows, width), k_s.dtype)
        v_s[pl.ds(0, rows), :] = jnp.zeros((rows, width), v_s.dtype)

    @pl.when(jnp.logical_not(has_next))
    def _():
        ret_in[...] = jnp.zeros(ret_in.shape, ret_in.dtype)

    fill_bias()
    for f in range(2):
        own_block(LEFT, f)
        own_block(RIGHT, f)
    for key in ("k", "v", "q"):
        loads[key].wait()
    own_block(FAR, 0)
    up_block(LEFT, 0)
    up_block(RIGHT, 0)

    @pl.when(has_prev)
    def _():
        arrive(halo())

    @pl.when(x == 0)
    def _():
        for s in range(4):
            grad_on(s).start()

    forward(0)
    start(att_own(0))
    own_block(FAR, 1)
    up_block(LEFT, 1)
    up_block(RIGHT, 1)
    forward(1)
    start(att_own(1))
    att_relay(0)
    up_block(FAR, 0)
    down_block(LEFT, 0)
    down_block(RIGHT, 0)
    forward(2)
    start(att_own(2))
    att_relay(1)
    up_block(FAR, 1)
    forward(3)
    start(att_own(3))
    att_relay(2)
    down_block(LEFT, 1)
    loads["w"].wait()
    loads["g"].wait()
    mate_blocks(0)
    d_out_terms(0)
    start(far_terms(0))
    start(plain_terms(0))
    att_relay(3)
    down_block(RIGHT, 1)
    down_block(FAR, 0)
    far_block(LEFT, 0)
    mate_blocks(1)
    d_out_terms(1)
    start(far_terms(1))
    start(plain_terms(1))
    far_block(RIGHT, 0)
    down_block(FAR, 1)
    far_block(FAR, 0)
    loads["s"].wait()
    for o in range(PAIRS):
        arrive(att_pass(o))
    mate_blocks(2)
    mate_blocks(3, (0,))
    rebuild(0)
    rebuild(1)
    merge(0)
    far_block(LEFT, 1)
    d_out_terms(2)
    start(far_terms(2))
    start(plain_terms(2))
    far_block(RIGHT, 1)
    far_block(FAR, 1)
    merge(1)
    mate_blocks(3, (1,))
    d_out_terms(3)
    start(far_terms(3))
    start(plain_terms(3))
    rebuild(2)
    d_out_done(0)
    merge(2)
    backward(0)
    rebuild(3)
    d_out_done(1)
    merge(3)
    backward(1)
    d_out_done(2)
    backward(2)
    relay_on(0)
    relay_on(1)
    d_out_done(3)
    backward(3)
    relay_on(2)

    chip_next = lax.rem(x + core, 4)
    pairs_next = [lax.rem(chip_next + n, 4) for n in (0, 1, 3, 2)]
    for o, p in enumerate(pairs_next):
        @pl.when(has_next)
        def _():
            arrive(back(p))

        cols = pl.ds(pl.multiple_of(p * pw, pw), pw)
        for i, (ref, out) in enumerate(((k_s, dk_hbm), (v_s, dv_hbm))):
            total = mine[i, p] + ret_in[i, p].astype(jnp.float32)
            ref[pl.ds(rows, rows), cols] = total.astype(jnp.bfloat16)
            local(ref.at[pl.ds(rows, rows), cols], out.at[0, :, cols], osem.at[1 + i, o]).start()

    for r in (LEFT, RIGHT, FAR):
        for f in range(2):
            w_first((4 - r) % 4, f).wait_send()
            w_up(r, f, x).wait_send()
            w_down(r, f, x).wait_send()
            w_far(r, f, xs[2] if (r, f) in upward else xs[1]).wait_send()
            for o in range(PAIRS):
                w_mate(r, f, o, core).wait_send()
    for o in range(PAIRS):
        sent(att_own(o))
        sent(att_pass(o))
        sent(far_terms(o))
        sent(plain_terms(o))
        sent(merged_terms(o))
        grad_on(o).wait_send()
        grad_on(o).wait_recv()
        stream_on(o).wait_send()
        stream_on(o).wait_recv()

    @pl.when(has_next)
    def _():
        sent(halo())

    @pl.when(has_prev)
    def _():
        sent(back(xs[3]))

    @pl.when(has_prev & jnp.logical_not(is_first))
    def _():
        for o in range(3):
            sent(back(xs[o]))

    @pl.when(is_first)
    def _():
        for o in range(3):
            sent(to_relay(o))

    @pl.when(is_relay)
    def _():
        sent(from_relay())

    for o, p in enumerate(pairs_next):
        local(dq_s.at[:, pair_rows(o)], dq_hbm.at[0, :, pair_rows(o)], osem.at[0, o]).wait()
        cols = pl.ds(pl.multiple_of(p * pw, pw), pw)
        for i, (ref, out) in enumerate(((k_s, dk_hbm), (v_s, dv_hbm))):
            local(ref.at[pl.ds(rows, rows), cols], out.at[0, :, cols], osem.at[1 + i, o]).wait()


def body(queries, keys, values, stream, grad_stream, out_proj, doc_ids):
    rows, width = queries.shape[1], queries.shape[2]
    shard = stream.shape[2]
    bf, f32 = jnp.bfloat16, jnp.float32
    qb, pw = rows // 2, 2 * HD
    dma = pltpu.SemaphoreType.DMA
    hbm = pl.BlockSpec(memory_space=pl.ANY)
    sizes = (lax.axis_size("ctx"), lax.axis_size("tp"), lax.axis_size("pipe"))
    assert sizes[0] % 8 == 0 and sizes[1] == 4 and rows == WINDOW and width == 8 * HD
    like = lambda x: jax.ShapeDtypeStruct(x.shape, x.dtype)
    return pl.pallas_call(
        functools.partial(kernel, rows, width, shard, *sizes),
        out_shape=(like(queries), like(keys), like(values), like(stream), like(grad_stream)),
        in_specs=[hbm] * 6 + [pl.BlockSpec(memory_space=pltpu.VMEM)],
        out_specs=(hbm,) * 5,
        scratch_shapes=[
            pltpu.VMEM((4, width, shard), bf),
            pltpu.VMEM((rows, shard), bf),
            pltpu.VMEM((rows, width), bf),
            pltpu.VMEM((2 * rows, width), bf),
            pltpu.VMEM((2 * rows, width), bf),
            pltpu.VMEM((rows, shard), bf),
            pltpu.VMEM((PAIRS, 4, pw, rows), bf),
            pltpu.VMEM((4, PAIRS, rows, pw), bf),
            pltpu.VMEM((PAIRS, pw, rows), bf),
            pltpu.VMEM((8, 2, 3 * qb, qb), bf),
            pltpu.VMEM((2, 3 * qb, qb), f32),
            pltpu.VMEM((rows, shard // 4), f32),
            pltpu.VMEM((2, PAIRS, rows, pw), bf),
            pltpu.VMEM((2, PAIRS, rows, pw), bf),
            pltpu.VMEM((2, rows, pw), bf),
            pltpu.VMEM((2, PAIRS, rows, pw), f32),
            pltpu.VMEM((rows, width), bf),
            pltpu.VMEM((PAIRS, pw, qb), bf),
            pltpu.VMEM((PAIRS, pw, qb), bf),
            pltpu.VMEM((PAIRS, pw, rows), bf),
            pltpu.VMEM((PAIRS, pw, rows), bf),
            dma((6,)), dma((3, 4)),
            dma((3, 2)), dma((3, 2)), dma((3, 3, 2)), dma((3, 3, 2)), dma((4, 3, 2)), dma((4, 3, 2)),
            dma((4, 4)), dma((4, 4)),
            dma((2,)), dma((2,)), dma((2, 5)), dma((2, 4)), dma((2, 3)), dma((2,)),
            dma((3, 2, 4)), dma((3, 2, 4)),
            dma((4,)), dma((4,)), dma((4,)), dma((4,)),
        ],
        compiler_params=pltpu.CompilerParams(
            collective_id=0, has_side_effects=True, vmem_limit_bytes=67043328
        ),
    )(queries, keys, values, stream, grad_stream, out_proj, doc_ids)


def solution(mesh):
    spec = P("pipe", "ctx", "tp")
    in_specs = (spec,) * 5 + (P("pipe", "tp", None), P("pipe", None))
    return jax.shard_map(body, mesh=mesh, in_specs=in_specs, out_specs=(spec,) * 5, check_vma=False)
```

```python
import functools
import math

import jax
import jax.numpy as jnp
from jax import lax
from jax.experimental import pallas as pl
from jax.experimental.pallas import tpu as pltpu
from jax.sharding import PartitionSpec as P

HD = 128
WINDOW = 512
NEG = -1e30
MESH = pl.DeviceIdType.MESH
NT = (((1,), (1,)), ((), ()))
OWN, RIGHT, FAR, LEFT = 0, 1, 2, 3
PAIRS = 4


def dot(a, b, dims=(((1,), (0,)), ((), ()))):
    return lax.dot_general(a, b, dims, preferred_element_type=jnp.float32)


def kernel(
    rows, width, shard, ctx_n, tp_n, pipe_n,
    q_hbm, k_hbm, v_hbm, s_hbm, g_hbm, w_hbm, doc_ref,
    dq_hbm, dk_hbm, dv_hbm, ns_hbm, ng_hbm,
    w_s, g_s, q_s, k_s, v_s, st_s, part, att, out_t, prob, bias,
    acc, ret_out, ret_in, relay, mine, dq_s, in_a, in_b, fin_l, fin_r,
    lsem, osem, w1s, w1r, wxs, wxr, wcs, wcr, ats, atr, hs, hr, rts, rtr, rls, rlr, rss, rsr, pgs, pgr, prs, prr,
):
    pipe = lax.axis_index("pipe")
    c = lax.axis_index("ctx")
    z = lax.axis_index("tp")
    nxt, prv = lax.rem(c + 1, ctx_n), lax.rem(c + ctx_n - 1, ctx_n)
    other = lax.rem(pipe + 1, pipe_n)
    has_prev, has_next = c > 0, c < ctx_n - 1
    qb, sub = rows // 2, rows // 4
    kw, pw = 3 * qb, 2 * HD
    row = c // 8
    x, core = lax.rem(c, 8) // 2, lax.rem(c, 2)
    mate = 1 - core
    xs = (x, lax.rem(x + 1, 4), lax.rem(x + 3, 4), lax.rem(x + 2, 4))

    def at_x(chip, side):
        return {"ctx": row * 8 + chip * 2 + side}

    to_z = {d: {"tp": lax.rem(z + d, tp_n)} for d in (RIGHT, FAR, LEFT)}
    x_up, x_down, x_mate = at_x(xs[1], core), at_x(xs[2], core), at_x(x, mate)

    barrier = pltpu.get_barrier_semaphore()
    partners = (*to_z.values(), x_up, x_down, x_mate, {"ctx": nxt}, {"ctx": prv}, {"pipe": other})
    for where in partners:
        pl.semaphore_signal(barrier, inc=1, device_id=where, device_id_type=MESH)

    more_rows = c < ctx_n - 8
    is_first = (lax.rem(c, 8) == 0) & has_prev
    is_relay = (core == 0) & (x < 3) & more_rows
    is_last = (lax.rem(c, 8) == 7) & more_rows
    row_last = {"ctx": row * 8 + 7}
    row_next = {"ctx": lax.rem(row * 8 + 8, ctx_n)}

    @pl.when(is_relay)
    def _():
        pl.semaphore_signal(barrier, inc=1, device_id=row_next, device_id_type=MESH)

    @pl.when(is_last)
    def _():
        for chip in range(3):
            pl.semaphore_signal(barrier, inc=1, device_id=at_x(chip, 0), device_id_type=MESH)

    def local(src, dst, sem):
        return pltpu.make_async_copy(src, dst, sem)

    def remote(src, dst, ssem, rsem, where):
        return pltpu.make_async_remote_copy(
            src_ref=src, dst_ref=dst, send_sem=ssem, recv_sem=rsem,
            device_id=where, device_id_type=MESH,
        )

    def features(d):
        return pl.ds(pl.multiple_of(lax.rem(z + d, tp_n) * shard, shard), shard)

    def block(chip, side):
        return pl.ds(pl.multiple_of((chip * 2 + side) * HD, HD), HD)

    def pair_rows(o):
        return pl.ds(pl.multiple_of(xs[o] * pw, pw), pw)

    loads = {
        "q": local(q_hbm.at[0], q_s, lsem.at[0]),
        "k": local(k_hbm.at[0], k_s.at[pl.ds(rows, rows)], lsem.at[1]),
        "v": local(v_hbm.at[0], v_s.at[pl.ds(rows, rows)], lsem.at[2]),
        "g": local(g_hbm.at[0], g_s, lsem.at[3]),
        "w": local(w_hbm.at[0, :, features(OWN)], w_s.at[OWN], lsem.at[4]),
        "s": local(s_hbm.at[0], st_s, lsem.at[5]),
    }

    part_f = shard // 2

    def w_first(d, f):
        there = (4 - d) % 4
        here = block(x, core)
        start_at = lax.rem(z + d, tp_n) * shard + f * part_f
        cols = pl.ds(pl.multiple_of(start_at, part_f), part_f)
        return remote(
            w_hbm.at[0, here, cols], w_s.at[there, here, pl.ds(f * part_f, part_f)],
            w1s.at[there - 1, f], w1r.at[there - 1, f], to_z[d],
        )

    def w_piece(r, f, chip, side, ssem, rsem, where):
        here = w_s.at[r, block(chip, side), pl.ds(f * part_f, part_f)]
        return remote(here, here, ssem, rsem, where)

    def w_up(r, f, chip):
        return w_piece(r, f, chip, core, wxs.at[0, r - 1, f], wxr.at[0, r - 1, f], x_up)

    def w_down(r, f, chip):
        return w_piece(r, f, chip, core, wxs.at[1, r - 1, f], wxr.at[1, r - 1, f], x_down)

    upward = ((RIGHT, 1), (FAR, 1))

    def w_far(r, f, chip):
        where = x_up if (r, f) in upward else x_down
        return w_piece(r, f, chip, core, wxs.at[2, r - 1, f], wxr.at[2, r - 1, f], where)

    def w_mate(r, f, o, side):
        return w_piece(r, f, xs[o], side, wcs.at[o, r - 1, f], wcr.at[o, r - 1, f], x_mate)

    def own_block(r, f):
        w_first((4 - r) % 4, f).wait_recv()
        own_block_on(r, f)

    def own_block_on(r, f):
        if r == FAR or f == 1:
            w_up(r, f, x).start()
        else:
            @pl.when(core == 1)
            def _():
                w_up(r, f, x).start()

        w_down(r, f, x).start()
        w_mate(r, f, 0, core).start()

    def up_block(r, f):
        w_down(r, f, xs[1]).wait_recv()
        if (r, f) not in upward:
            w_far(r, f, xs[1]).start()
        w_mate(r, f, 1, core).start()

    def down_block(r, f):
        w_up(r, f, xs[2]).wait_recv()
        if (r, f) in upward:
            w_far(r, f, xs[2]).start()
        w_mate(r, f, 2, core).start()

    def far_block(r, f):
        w_far(r, f, xs[3]).wait_recv()
        w_mate(r, f, 3, core).start()

    def mate_blocks(o, halves=(0, 1)):
        for f in halves:
            for r in (LEFT, RIGHT, FAR):
                w_mate(r, f, o, mate).wait_recv()

    lo, hi = pl.ds(0, qb), pl.ds(qb, qb)

    def att_own(o):
        return (
            remote(att.at[OWN, o], att.at[LEFT, o], ats.at[0, o], atr.at[0, o], to_z[RIGHT]),
            remote(att.at[OWN, o], att.at[RIGHT, o], ats.at[1, o], atr.at[1, o], to_z[LEFT]),
        )

    def att_pass(o):
        return (
            remote(att.at[LEFT, o, lo], att.at[FAR, o, lo], ats.at[2, o], atr.at[2, o], to_z[RIGHT]),
            remote(att.at[RIGHT, o, hi], att.at[FAR, o, hi], ats.at[3, o], atr.at[3, o], to_z[LEFT]),
        )

    def far_terms(o):
        return (
            remote(part.at[o, FAR, :, lo], in_a.at[o], rss.at[0, 0, o], rsr.at[0, 0, o], to_z[RIGHT]),
            remote(part.at[o, FAR, :, hi], in_b.at[o], rss.at[0, 1, o], rsr.at[0, 1, o], to_z[LEFT]),
        )

    def plain_terms(o):
        return (
            remote(part.at[o, RIGHT, :, hi], fin_l.at[o, :, hi], rss.at[1, 0, o], rsr.at[1, 0, o], to_z[RIGHT]),
            remote(part.at[o, LEFT, :, lo], fin_r.at[o, :, lo], rss.at[1, 1, o], rsr.at[1, 1, o], to_z[LEFT]),
        )

    def merged_terms(o):
        return (
            remote(part.at[o, RIGHT, :, lo], fin_l.at[o, :, lo], rss.at[2, 0, o], rsr.at[2, 0, o], to_z[RIGHT]),
            remote(part.at[o, LEFT, :, hi], fin_r.at[o, :, hi], rss.at[2, 1, o], rsr.at[2, 1, o], to_z[LEFT]),
        )

    def halo():
        return (
            remote(k_hbm.at[0], k_s.at[pl.ds(0, rows)], hs.at[0], hr.at[0], {"ctx": nxt}),
            remote(v_hbm.at[0], v_s.at[pl.ds(0, rows)], hs.at[1], hr.at[1], {"ctx": nxt}),
        )

    def back(p):
        return tuple(
            remote(ret_out.at[i, p], ret_in.at[i, p], rts.at[i, p], rtr.at[i, p], {"ctx": prv})
            for i in range(2)
        )

    def to_relay(o):
        where = {"ctx": jnp.maximum(row - 1, 0) * 8 + o * 2}
        return tuple(
            remote(ret_out.at[i, xs[o]], relay.at[i], rls.at[i, o], rlr.at[i], where)
            for i in range(2)
        )

    def from_relay():
        p = x + x // 2
        return tuple(
            remote(relay.at[i], ret_in.at[i, p], rts.at[i, 4], rtr.at[i, p], row_last)
            for i in range(2)
        )

    def relay_on(chip):
        @pl.when(is_relay & (x == chip))
        def _():
            arrive(tuple(
                remote(ret_out.at[i, 0], relay.at[i], rls.at[i, 0], rlr.at[i], row_next) for i in range(2)
            ))
            start(from_relay())

    def grad_on(s):
        here = pl.ds(s * sub, sub)
        return remote(g_hbm.at[0, here], ng_hbm.at[0, here], pgs.at[s], pgr.at[s], {"pipe": other})

    wide = shard // 4

    def stream_on(n):
        cols = pl.ds(n * wide, wide)
        return remote(st_s.at[:, cols], ns_hbm.at[0, :, cols], prs.at[n], prr.at[n], {"pipe": other})

    def start(copies):
        for copy in copies:
            copy.start()

    def arrive(copies):
        for copy in copies:
            copy.wait_recv()

    def sent(copies):
        for copy in copies:
            copy.wait_send()

    def fill_bias():
        own_doc = doc_ref[:, pl.ds(pl.multiple_of(c * rows, rows), rows)].astype(jnp.float32)
        old_doc = doc_ref[:, pl.ds(pl.multiple_of(jnp.maximum(c - 1, 0) * rows, rows), rows)].astype(jnp.float32)
        key_doc = jnp.transpose(jnp.broadcast_to(jnp.concatenate([old_doc, own_doc], axis=1), (HD, 2 * rows)))
        a = lax.broadcasted_iota(jnp.int32, (kw, qb), 0)
        b = lax.broadcasted_iota(jnp.int32, (kw, qb), 1)
        for t in range(2):
            seen = (a <= b + rows) & (a > b + (rows - WINDOW))
            seen = seen & ((a + t * qb >= rows) | has_prev)
            columns = jnp.broadcast_to(key_doc[t * qb:t * qb + kw, :1], (kw, qb))
            seen = seen & (columns == own_doc[:, t * qb:(t + 1) * qb])
            bias[t] = jnp.where(seen, 0.0, NEG)

    scaling = HD ** -0.5

    def forward(o):
        def step(i, _):
            cols = pl.ds(pl.multiple_of(xs[o] * pw + i * HD, HD), HD)
            mine_cols = pl.ds(pl.multiple_of(i * HD, HD), HD)
            for t in range(2):
                tokens = pl.ds(t * qb, qb)
                keys = k_s[pl.ds(t * qb, kw), cols]
                values = v_s[pl.ds(t * qb, kw), cols]
                scores = dot(keys, q_s[tokens, cols], NT) + bias[t]
                top = jnp.max(scores, axis=0, keepdims=True)
                exponent = jnp.exp2((scores - top) * (scaling * math.log2(math.e)))
                total = jnp.sum(exponent, axis=0, keepdims=True)
                weights = (exponent * (1.0 / total)).astype(jnp.bfloat16)
                prob[o * 2 + i, t] = weights
                out = dot(jnp.transpose(values), weights)
                out_t[o, mine_cols, tokens] = out.astype(jnp.bfloat16)
                att[OWN, o, tokens, mine_cols] = jnp.transpose(out).astype(jnp.bfloat16)
            return 0

        lax.fori_loop(0, 2, step, 0)

    def d_out_terms(o):
        def step(r, _):
            term = dot(w_s[r, pair_rows(o), :], g_s[...], NT)
            part[o, r] = term.astype(jnp.bfloat16)
            return 0

        lax.fori_loop(0, 4, step, 0)

    def add_into(r, o, cols, extra):
        part[o, r, :, cols] = (
            part[o, r, :, cols].astype(jnp.float32) + extra.astype(jnp.float32)
        ).astype(jnp.bfloat16)

    def merge(o):
        arrive(far_terms(o))
        add_into(RIGHT, o, lo, in_a[o])
        add_into(LEFT, o, hi, in_b[o])
        start(merged_terms(o))

    def d_out_done(o):
        arrive(plain_terms(o))
        arrive(merged_terms(o))
        total = part[o, OWN].astype(jnp.float32) + fin_l[o].astype(jnp.float32) + fin_r[o].astype(jnp.float32)
        part[o, OWN] = total.astype(jnp.bfloat16)

    def backward(o):
        def step(i, _):
            cols = pl.ds(pl.multiple_of(xs[o] * pw + i * HD, HD), HD)
            mine_cols = pl.ds(pl.multiple_of(i * HD, HD), HD)
            d_keys, d_values = [], []
            for t in range(2):
                tokens = pl.ds(t * qb, qb)
                keys = k_s[pl.ds(t * qb, kw), cols]
                values = v_s[pl.ds(t * qb, kw), cols]
                queries = q_s[tokens, cols]
                d_out = part[o, OWN, mine_cols, tokens]
                weights = prob[o * 2 + i, t]
                delta = jnp.sum(
                    d_out.astype(jnp.float32) * out_t[o, mine_cols, tokens].astype(jnp.float32),
                    axis=0, keepdims=True,
                )
                d_prob = dot(values, d_out)
                d_score = (weights.astype(jnp.float32) * (d_prob - delta)).astype(jnp.bfloat16)
                d_values.append(dot(weights, d_out, NT))
                d_keys.append(dot(d_score, queries) * scaling)
                d_query = dot(jnp.transpose(keys), d_score) * scaling
                dq_s[tokens, cols] = jnp.transpose(d_query).astype(jnp.bfloat16)
            for n, (early, late) in enumerate((d_keys, d_values)):
                ret_out[n, xs[o], pl.ds(0, qb), mine_cols] = early[:qb].astype(jnp.bfloat16)
                ret_out[n, xs[o], pl.ds(qb, qb), mine_cols] = (early[qb:2 * qb] + late[:qb]).astype(jnp.bfloat16)
                mine[n, xs[o], pl.ds(0, qb), mine_cols] = early[2 * qb:] + late[qb:2 * qb]
                mine[n, xs[o], pl.ds(qb, qb), mine_cols] = late[2 * qb:]
            return 0

        lax.fori_loop(0, 2, step, 0)

        @pl.when(has_prev if o == 3 else has_prev & jnp.logical_not(is_first))
        def _():
            start(back(xs[o]))

        if o < 3:
            @pl.when(is_first)
            def _():
                start(to_relay(o))

        local(dq_s.at[:, pair_rows(o)], dq_hbm.at[0, :, pair_rows(o)], osem.at[0, o]).start()

    def rebuild(n):
        cols = pl.ds(n * wide, wide)

        def step(o, _):
            pair = lax.rem(x + o + o // 2 - 2 * (o // 3), 4)
            heads = pl.ds(pl.multiple_of(pair * pw, pw), pw)
            left = jnp.concatenate([att[r, o] for r in range(4)], axis=1)
            term = dot(left, w_s[:, heads, cols].reshape(4 * pw, wide))

            @pl.when(o == 0)
            def _():
                acc[...] = term

            @pl.when(o > 0)
            def _():
                acc[...] += term

            return 0

        lax.fori_loop(0, PAIRS, step, 0)
        st_s[:, cols] = (st_s[:, cols].astype(jnp.float32) - acc[...]).astype(jnp.bfloat16)
        stream_on(n).start()

    def att_relay(o):
        arrive(att_own(o))
        start(att_pass(o))

    for key in ("k", "v", "q", "w", "g", "s"):
        loads[key].start()

    awaited = len(partners) + jnp.where(is_first, 3, 0) + jnp.where(is_relay, 1, 0)
    pl.semaphore_wait(barrier, awaited)
    for f in range(2):
        w_first(RIGHT, f).start()
        w_first(LEFT, f).start()

    @pl.when(has_next)
    def _():
        start(halo())

    for f in range(2):
        w_first(FAR, f).start()

    @pl.when(x > 0)
    def _():
        for s in range(4):
            grad_on(s).start()

    @pl.when(jnp.logical_not(has_prev))
    def _():
        k_s[pl.ds(0, rows), :] = jnp.zeros((rows, width), k_s.dtype)
        v_s[pl.ds(0, rows), :] = jnp.zeros((rows, width), v_s.dtype)

    @pl.when(jnp.logical_not(has_next))
    def _():
        ret_in[...] = jnp.zeros(ret_in.shape, ret_in.dtype)

    fill_bias()
    own_block(LEFT, 0)
    own_block(RIGHT, 0)
    for key in ("k", "v", "q"):
        loads[key].wait()
    w_first(FAR, 0).wait_recv()

    @pl.when(core == 0)
    def _():
        w_up(LEFT, 0, x).start()
        w_up(RIGHT, 0, x).start()

    own_block_on(FAR, 0)
    up_block(LEFT, 0)
    up_block(RIGHT, 0)

    @pl.when(has_prev)
    def _():
        arrive(halo())

    @pl.when(x == 0)
    def _():
        for s in range(4):
            grad_on(s).start()

    forward(0)
    start(att_own(0))
    up_block(FAR, 0)
    own_block(LEFT, 1)
    own_block(RIGHT, 1)
    own_block(FAR, 1)
    forward(1)
    start(att_own(1))
    down_block(LEFT, 0)
    att_relay(0)
    forward(2)
    start(att_own(2))
    down_block(RIGHT, 0)
    att_relay(1)
    forward(3)
    start(att_own(3))
    down_block(FAR, 0)
    far_block(LEFT, 0)
    far_block(RIGHT, 0)
    att_relay(2)
    loads["w"].wait()
    loads["g"].wait()
    mate_blocks(0)
    d_out_terms(0)
    start(far_terms(0))
    start(plain_terms(0))
    att_relay(3)
    up_block(LEFT, 1)
    far_block(FAR, 0)
    down_block(LEFT, 1)
    up_block(RIGHT, 1)
    down_block(RIGHT, 1)
    loads["s"].wait()
    for o in range(1, PAIRS):
        mate_blocks(o, (0,))
    up_block(FAR, 1)
    for o in range(PAIRS):
        arrive(att_pass(o))
    rebuild(0)
    down_block(FAR, 1)
    mate_blocks(1, (1,))
    d_out_terms(1)
    start(far_terms(1))
    start(plain_terms(1))
    far_block(LEFT, 1)
    mate_blocks(2, (1,))
    d_out_terms(2)
    start(far_terms(2))
    start(plain_terms(2))
    rebuild(1)
    far_block(RIGHT, 1)
    far_block(FAR, 1)
    merge(0)
    mate_blocks(3, (1,))
    d_out_terms(3)
    start(far_terms(3))
    start(plain_terms(3))
    merge(1)
    rebuild(2)
    d_out_done(0)
    merge(2)
    backward(0)
    rebuild(3)
    d_out_done(1)
    merge(3)
    backward(1)
    d_out_done(2)
    backward(2)
    relay_on(0)
    relay_on(1)
    d_out_done(3)
    backward(3)
    relay_on(2)

    chip_next = lax.rem(x + core, 4)
    pairs_next = [lax.rem(chip_next + n, 4) for n in (0, 1, 3, 2)]
    for o, p in enumerate(pairs_next):
        @pl.when(has_next)
        def _():
            arrive(back(p))

        cols = pl.ds(pl.multiple_of(p * pw, pw), pw)
        for i, (ref, out) in enumerate(((k_s, dk_hbm), (v_s, dv_hbm))):
            total = mine[i, p] + ret_in[i, p].astype(jnp.float32)
            ref[pl.ds(rows, rows), cols] = total.astype(jnp.bfloat16)
            local(ref.at[pl.ds(rows, rows), cols], out.at[0, :, cols], osem.at[1 + i, o]).start()

    for r in (LEFT, RIGHT, FAR):
        for f in range(2):
            w_first((4 - r) % 4, f).wait_send()
            w_up(r, f, x).wait_send()
            w_down(r, f, x).wait_send()
            w_far(r, f, xs[2] if (r, f) in upward else xs[1]).wait_send()
            for o in range(PAIRS):
                w_mate(r, f, o, core).wait_send()
    for o in range(PAIRS):
        sent(att_own(o))
        sent(att_pass(o))
        sent(far_terms(o))
        sent(plain_terms(o))
        sent(merged_terms(o))
        grad_on(o).wait_send()
        grad_on(o).wait_recv()
        stream_on(o).wait_send()
        stream_on(o).wait_recv()

    @pl.when(has_next)
    def _():
        sent(halo())

    @pl.when(has_prev)
    def _():
        sent(back(xs[3]))

    @pl.when(has_prev & jnp.logical_not(is_first))
    def _():
        for o in range(3):
            sent(back(xs[o]))

    @pl.when(is_first)
    def _():
        for o in range(3):
            sent(to_relay(o))

    @pl.when(is_relay)
    def _():
        sent(from_relay())

    for o, p in enumerate(pairs_next):
        local(dq_s.at[:, pair_rows(o)], dq_hbm.at[0, :, pair_rows(o)], osem.at[0, o]).wait()
        cols = pl.ds(pl.multiple_of(p * pw, pw), pw)
        for i, (ref, out) in enumerate(((k_s, dk_hbm), (v_s, dv_hbm))):
            local(ref.at[pl.ds(rows, rows), cols], out.at[0, :, cols], osem.at[1 + i, o]).wait()


def body(queries, keys, values, stream, grad_stream, out_proj, doc_ids):
    rows, width = queries.shape[1], queries.shape[2]
    shard = stream.shape[2]
    bf, f32 = jnp.bfloat16, jnp.float32
    qb, pw = rows // 2, 2 * HD
    dma = pltpu.SemaphoreType.DMA
    hbm = pl.BlockSpec(memory_space=pl.ANY)
    sizes = (lax.axis_size("ctx"), lax.axis_size("tp"), lax.axis_size("pipe"))
    assert sizes[0] % 8 == 0 and sizes[1] == 4 and rows == WINDOW and width == 8 * HD
    like = lambda x: jax.ShapeDtypeStruct(x.shape, x.dtype)
    return pl.pallas_call(
        functools.partial(kernel, rows, width, shard, *sizes),
        out_shape=(like(queries), like(keys), like(values), like(stream), like(grad_stream)),
        in_specs=[hbm] * 6 + [pl.BlockSpec(memory_space=pltpu.VMEM)],
        out_specs=(hbm,) * 5,
        scratch_shapes=[
            pltpu.VMEM((4, width, shard), bf),
            pltpu.VMEM((rows, shard), bf),
            pltpu.VMEM((rows, width), bf),
            pltpu.VMEM((2 * rows, width), bf),
            pltpu.VMEM((2 * rows, width), bf),
            pltpu.VMEM((rows, shard), bf),
            pltpu.VMEM((PAIRS, 4, pw, rows), bf),
            pltpu.VMEM((4, PAIRS, rows, pw), bf),
            pltpu.VMEM((PAIRS, pw, rows), bf),
            pltpu.VMEM((8, 2, 3 * qb, qb), bf),
            pltpu.VMEM((2, 3 * qb, qb), f32),
            pltpu.VMEM((rows, shard // 4), f32),
            pltpu.VMEM((2, PAIRS, rows, pw), bf),
            pltpu.VMEM((2, PAIRS, rows, pw), bf),
            pltpu.VMEM((2, rows, pw), bf),
            pltpu.VMEM((2, PAIRS, rows, pw), f32),
            pltpu.VMEM((rows, width), bf),
            pltpu.VMEM((PAIRS, pw, qb), bf),
            pltpu.VMEM((PAIRS, pw, qb), bf),
            pltpu.VMEM((PAIRS, pw, rows), bf),
            pltpu.VMEM((PAIRS, pw, rows), bf),
            dma((6,)), dma((3, 4)),
            dma((3, 2)), dma((3, 2)), dma((3, 3, 2)), dma((3, 3, 2)), dma((4, 3, 2)), dma((4, 3, 2)),
            dma((4, 4)), dma((4, 4)),
            dma((2,)), dma((2,)), dma((2, 5)), dma((2, 4)), dma((2, 3)), dma((2,)),
            dma((3, 2, 4)), dma((3, 2, 4)),
            dma((4,)), dma((4,)), dma((4,)), dma((4,)),
        ],
        compiler_params=pltpu.CompilerParams(
            collective_id=0, has_side_effects=True, vmem_limit_bytes=67043328
        ),
    )(queries, keys, values, stream, grad_stream, out_proj, doc_ids)


def solution(mesh):
    spec = P("pipe", "ctx", "tp")
    in_specs = (spec,) * 5 + (P("pipe", "tp", None), P("pipe", None))
    return jax.shard_map(body, mesh=mesh, in_specs=in_specs, out_specs=(spec,) * 5, check_vma=False)
```

```python
import functools
import math

import jax
import jax.numpy as jnp
from jax import lax
from jax.experimental import pallas as pl
from jax.experimental.pallas import tpu as pltpu
from jax.sharding import PartitionSpec as P

HD = 128
WINDOW = 512
NEG = -1e30
MESH = pl.DeviceIdType.MESH
NT = (((1,), (1,)), ((), ()))
OWN, RIGHT, FAR, LEFT = 0, 1, 2, 3
PAIRS = 4


def dot(a, b, dims=(((1,), (0,)), ((), ()))):
    return lax.dot_general(a, b, dims, preferred_element_type=jnp.float32)


def kernel(
    rows, width, shard, ctx_n, tp_n, pipe_n,
    q_hbm, k_hbm, v_hbm, s_hbm, g_hbm, w_hbm, doc_ref,
    dq_hbm, dk_hbm, dv_hbm, ns_hbm, ng_hbm,
    w_s, g_s, q_s, k_s, v_s, st_s, part, att, out_t, prob, bias,
    acc, ret_out, ret_in, relay, mine, dq_s, in_a, in_b, fin_l, fin_r,
    lsem, osem, w1s, w1r, wxs, wxr, wcs, wcr, ats, atr, hs, hr, rts, rtr, rls, rlr, rss, rsr, pgs, pgr, prs, prr,
):
    pipe = lax.axis_index("pipe")
    c = lax.axis_index("ctx")
    z = lax.axis_index("tp")
    nxt, prv = lax.rem(c + 1, ctx_n), lax.rem(c + ctx_n - 1, ctx_n)
    other = lax.rem(pipe + 1, pipe_n)
    has_prev, has_next = c > 0, c < ctx_n - 1
    qb, sub = rows // 2, rows // 4
    kw, pw = 3 * qb, 2 * HD
    row = c // 8
    x, core = lax.rem(c, 8) // 2, lax.rem(c, 2)
    mate = 1 - core
    xs = (x, lax.rem(x + 1, 4), lax.rem(x + 3, 4), lax.rem(x + 2, 4))

    def at_x(chip, side):
        return {"ctx": row * 8 + chip * 2 + side}

    to_z = {d: {"tp": lax.rem(z + d, tp_n)} for d in (RIGHT, FAR, LEFT)}
    x_up, x_down, x_mate = at_x(xs[1], core), at_x(xs[2], core), at_x(x, mate)

    barrier = pltpu.get_barrier_semaphore()
    partners = (*to_z.values(), x_up, x_down, x_mate, {"ctx": nxt}, {"ctx": prv}, {"pipe": other})
    for where in partners:
        pl.semaphore_signal(barrier, inc=1, device_id=where, device_id_type=MESH)

    more_rows = c < ctx_n - 8
    is_first = (lax.rem(c, 8) == 0) & has_prev
    is_relay = (core == 0) & (x < 3) & more_rows
    is_last = (lax.rem(c, 8) == 7) & more_rows
    row_last = {"ctx": row * 8 + 7}
    row_next = {"ctx": lax.rem(row * 8 + 8, ctx_n)}

    @pl.when(is_relay)
    def _():
        pl.semaphore_signal(barrier, inc=1, device_id=row_next, device_id_type=MESH)

    @pl.when(is_last)
    def _():
        for chip in range(3):
            pl.semaphore_signal(barrier, inc=1, device_id=at_x(chip, 0), device_id_type=MESH)

    def local(src, dst, sem):
        return pltpu.make_async_copy(src, dst, sem)

    def remote(src, dst, ssem, rsem, where):
        return pltpu.make_async_remote_copy(
            src_ref=src, dst_ref=dst, send_sem=ssem, recv_sem=rsem,
            device_id=where, device_id_type=MESH,
        )

    def features(d):
        return pl.ds(pl.multiple_of(lax.rem(z + d, tp_n) * shard, shard), shard)

    def block(chip, side):
        return pl.ds(pl.multiple_of((chip * 2 + side) * HD, HD), HD)

    def pair_rows(o):
        return pl.ds(pl.multiple_of(xs[o] * pw, pw), pw)

    loads = {
        "q": local(q_hbm.at[0], q_s, lsem.at[0]),
        "k": local(k_hbm.at[0], k_s.at[pl.ds(rows, rows)], lsem.at[1]),
        "v": local(v_hbm.at[0], v_s.at[pl.ds(rows, rows)], lsem.at[2]),
        "g": local(g_hbm.at[0], g_s, lsem.at[3]),
        "w": local(w_hbm.at[0, :, features(OWN)], w_s.at[OWN], lsem.at[4]),
        "s": local(s_hbm.at[0], st_s, lsem.at[5]),
    }

    part_f = shard // 2

    def w_first(d, f):
        there = (4 - d) % 4
        here = block(x, core)
        start_at = lax.rem(z + d, tp_n) * shard + f * part_f
        cols = pl.ds(pl.multiple_of(start_at, part_f), part_f)
        return remote(
            w_hbm.at[0, here, cols], w_s.at[there, here, pl.ds(f * part_f, part_f)],
            w1s.at[there - 1, f], w1r.at[there - 1, f], to_z[d],
        )

    def w_piece(r, f, chip, side, ssem, rsem, where):
        here = w_s.at[r, block(chip, side), pl.ds(f * part_f, part_f)]
        return remote(here, here, ssem, rsem, where)

    def w_up(r, f, chip):
        return w_piece(r, f, chip, core, wxs.at[0, r - 1, f], wxr.at[0, r - 1, f], x_up)

    def w_down(r, f, chip):
        return w_piece(r, f, chip, core, wxs.at[1, r - 1, f], wxr.at[1, r - 1, f], x_down)

    upward = ((RIGHT, 1), (FAR, 1))

    def w_far(r, f, chip):
        where = x_up if (r, f) in upward else x_down
        return w_piece(r, f, chip, core, wxs.at[2, r - 1, f], wxr.at[2, r - 1, f], where)

    def w_mate(r, f, o, side):
        return w_piece(r, f, xs[o], side, wcs.at[o, r - 1, f], wcr.at[o, r - 1, f], x_mate)

    def own_block(r, f):
        w_first((4 - r) % 4, f).wait_recv()
        own_block_on(r, f)

    def own_block_on(r, f):
        if r == FAR or f == 1:
            w_up(r, f, x).start()
        else:
            @pl.when(core == 1)
            def _():
                w_up(r, f, x).start()

        w_down(r, f, x).start()
        w_mate(r, f, 0, core).start()

    def up_block(r, f):
        w_down(r, f, xs[1]).wait_recv()
        if (r, f) not in upward:
            w_far(r, f, xs[1]).start()
        w_mate(r, f, 1, core).start()

    def down_block(r, f):
        w_up(r, f, xs[2]).wait_recv()
        if (r, f) in upward:
            w_far(r, f, xs[2]).start()
        w_mate(r, f, 2, core).start()

    def far_block(r, f):
        w_far(r, f, xs[3]).wait_recv()
        w_mate(r, f, 3, core).start()

    def mate_blocks(o, halves=(0, 1)):
        for f in halves:
            for r in (LEFT, RIGHT, FAR):
                w_mate(r, f, o, mate).wait_recv()

    lo, hi = pl.ds(0, qb), pl.ds(qb, qb)

    def att_own(o):
        return (
            remote(att.at[OWN, o], att.at[LEFT, o], ats.at[0, o], atr.at[0, o], to_z[RIGHT]),
            remote(att.at[OWN, o], att.at[RIGHT, o], ats.at[1, o], atr.at[1, o], to_z[LEFT]),
        )

    def att_pass(o):
        return (
            remote(att.at[LEFT, o, lo], att.at[FAR, o, lo], ats.at[2, o], atr.at[2, o], to_z[RIGHT]),
            remote(att.at[RIGHT, o, hi], att.at[FAR, o, hi], ats.at[3, o], atr.at[3, o], to_z[LEFT]),
        )

    def far_terms(o):
        return (
            remote(part.at[o, FAR, :, lo], in_a.at[o], rss.at[0, 0, o], rsr.at[0, 0, o], to_z[RIGHT]),
            remote(part.at[o, FAR, :, hi], in_b.at[o], rss.at[0, 1, o], rsr.at[0, 1, o], to_z[LEFT]),
        )

    def plain_terms(o):
        return (
            remote(part.at[o, RIGHT, :, hi], fin_l.at[o, :, hi], rss.at[1, 0, o], rsr.at[1, 0, o], to_z[RIGHT]),
            remote(part.at[o, LEFT, :, lo], fin_r.at[o, :, lo], rss.at[1, 1, o], rsr.at[1, 1, o], to_z[LEFT]),
        )

    def merged_terms(o):
        return (
            remote(part.at[o, RIGHT, :, lo], fin_l.at[o, :, lo], rss.at[2, 0, o], rsr.at[2, 0, o], to_z[RIGHT]),
            remote(part.at[o, LEFT, :, hi], fin_r.at[o, :, hi], rss.at[2, 1, o], rsr.at[2, 1, o], to_z[LEFT]),
        )

    def halo():
        return (
            remote(k_hbm.at[0], k_s.at[pl.ds(0, rows)], hs.at[0], hr.at[0], {"ctx": nxt}),
            remote(v_hbm.at[0], v_s.at[pl.ds(0, rows)], hs.at[1], hr.at[1], {"ctx": nxt}),
        )

    def back(p):
        return tuple(
            remote(ret_out.at[i, p], ret_in.at[i, p], rts.at[i, p], rtr.at[i, p], {"ctx": prv})
            for i in range(2)
        )

    def to_relay(o):
        where = {"ctx": jnp.maximum(row - 1, 0) * 8 + o * 2}
        return tuple(
            remote(ret_out.at[i, xs[o]], relay.at[i], rls.at[i, o], rlr.at[i], where)
            for i in range(2)
        )

    def from_relay():
        p = x + x // 2
        return tuple(
            remote(relay.at[i], ret_in.at[i, p], rts.at[i, 4], rtr.at[i, p], row_last)
            for i in range(2)
        )

    def relay_on(chip):
        @pl.when(is_relay & (x == chip))
        def _():
            arrive(tuple(
                remote(ret_out.at[i, 0], relay.at[i], rls.at[i, 0], rlr.at[i], row_next) for i in range(2)
            ))
            start(from_relay())

    def grad_on(s):
        here = pl.ds(s * sub, sub)
        return remote(g_hbm.at[0, here], ng_hbm.at[0, here], pgs.at[s], pgr.at[s], {"pipe": other})

    wide = shard // 4

    def stream_on(n):
        cols = pl.ds(n * wide, wide)
        return remote(st_s.at[:, cols], ns_hbm.at[0, :, cols], prs.at[n], prr.at[n], {"pipe": other})

    def start(copies):
        for copy in copies:
            copy.start()

    def arrive(copies):
        for copy in copies:
            copy.wait_recv()

    def sent(copies):
        for copy in copies:
            copy.wait_send()

    def fill_bias():
        own_doc = doc_ref[:, pl.ds(pl.multiple_of(c * rows, rows), rows)].astype(jnp.float32)
        old_doc = doc_ref[:, pl.ds(pl.multiple_of(jnp.maximum(c - 1, 0) * rows, rows), rows)].astype(jnp.float32)
        key_doc = jnp.transpose(jnp.broadcast_to(jnp.concatenate([old_doc, own_doc], axis=1), (HD, 2 * rows)))
        a = lax.broadcasted_iota(jnp.int32, (kw, qb), 0)
        b = lax.broadcasted_iota(jnp.int32, (kw, qb), 1)
        for t in range(2):
            seen = (a <= b + rows) & (a > b + (rows - WINDOW))
            seen = seen & ((a + t * qb >= rows) | has_prev)
            columns = jnp.broadcast_to(key_doc[t * qb:t * qb + kw, :1], (kw, qb))
            seen = seen & (columns == own_doc[:, t * qb:(t + 1) * qb])
            bias[t] = jnp.where(seen, 0.0, NEG)

    scaling = HD ** -0.5

    def forward(o):
        def step(i, _):
            cols = pl.ds(pl.multiple_of(xs[o] * pw + i * HD, HD), HD)
            mine_cols = pl.ds(pl.multiple_of(i * HD, HD), HD)
            for t in range(2):
                tokens = pl.ds(t * qb, qb)
                keys = k_s[pl.ds(t * qb, kw), cols]
                values = v_s[pl.ds(t * qb, kw), cols]
                scores = dot(keys, q_s[tokens, cols], NT) + bias[t]
                top = jnp.max(scores, axis=0, keepdims=True)
                exponent = jnp.exp2((scores - top) * (scaling * math.log2(math.e)))
                total = jnp.sum(exponent, axis=0, keepdims=True)
                weights = (exponent * (1.0 / total)).astype(jnp.bfloat16)
                prob[o * 2 + i, t] = weights
                out = dot(jnp.transpose(values), weights)
                out_t[o, mine_cols, tokens] = out.astype(jnp.bfloat16)
                att[OWN, o, tokens, mine_cols] = jnp.transpose(out).astype(jnp.bfloat16)
            return 0

        lax.fori_loop(0, 2, step, 0)

    def d_out_terms(o):
        def step(r, _):
            term = dot(w_s[r, pair_rows(o), :], g_s[...], NT)
            part[o, r] = term.astype(jnp.bfloat16)
            return 0

        lax.fori_loop(0, 4, step, 0)

    def add_into(r, o, cols, extra):
        part[o, r, :, cols] = (
            part[o, r, :, cols].astype(jnp.float32) + extra.astype(jnp.float32)
        ).astype(jnp.bfloat16)

    def merge(o):
        arrive(far_terms(o))
        add_into(RIGHT, o, lo, in_a[o])
        add_into(LEFT, o, hi, in_b[o])
        start(merged_terms(o))

    def d_out_done(o):
        arrive(plain_terms(o))
        arrive(merged_terms(o))
        total = part[o, OWN].astype(jnp.float32) + fin_l[o].astype(jnp.float32) + fin_r[o].astype(jnp.float32)
        part[o, OWN] = total.astype(jnp.bfloat16)

    def backward(o):
        def step(i, _):
            cols = pl.ds(pl.multiple_of(xs[o] * pw + i * HD, HD), HD)
            mine_cols = pl.ds(pl.multiple_of(i * HD, HD), HD)
            d_keys, d_values = [], []
            for t in range(2):
                tokens = pl.ds(t * qb, qb)
                keys = k_s[pl.ds(t * qb, kw), cols]
                values = v_s[pl.ds(t * qb, kw), cols]
                queries = q_s[tokens, cols]
                d_out = part[o, OWN, mine_cols, tokens]
                weights = prob[o * 2 + i, t]
                delta = jnp.sum(
                    d_out.astype(jnp.float32) * out_t[o, mine_cols, tokens].astype(jnp.float32),
                    axis=0, keepdims=True,
                )
                d_prob = dot(values, d_out)
                d_score = (weights.astype(jnp.float32) * (d_prob - delta)).astype(jnp.bfloat16)
                d_values.append(dot(weights, d_out, NT))
                d_keys.append(dot(d_score, queries) * scaling)
                d_query = dot(jnp.transpose(keys), d_score) * scaling
                dq_s[tokens, cols] = jnp.transpose(d_query).astype(jnp.bfloat16)
            for n, (early, late) in enumerate((d_keys, d_values)):
                ret_out[n, xs[o], pl.ds(0, qb), mine_cols] = early[:qb].astype(jnp.bfloat16)
                ret_out[n, xs[o], pl.ds(qb, qb), mine_cols] = (early[qb:2 * qb] + late[:qb]).astype(jnp.bfloat16)
                mine[n, xs[o], pl.ds(0, qb), mine_cols] = early[2 * qb:] + late[qb:2 * qb]
                mine[n, xs[o], pl.ds(qb, qb), mine_cols] = late[2 * qb:]
            return 0

        lax.fori_loop(0, 2, step, 0)

        @pl.when(has_prev if o == 3 else has_prev & jnp.logical_not(is_first))
        def _():
            start(back(xs[o]))

        if o < 3:
            @pl.when(is_first)
            def _():
                start(to_relay(o))

        local(dq_s.at[:, pair_rows(o)], dq_hbm.at[0, :, pair_rows(o)], osem.at[0, o]).start()

    def rebuild(n):
        cols = pl.ds(n * wide, wide)

        def step(o, _):
            pair = lax.rem(x + o + o // 2 - 2 * (o // 3), 4)
            heads = pl.ds(pl.multiple_of(pair * pw, pw), pw)
            left = jnp.concatenate([att[r, o] for r in range(4)], axis=1)
            term = dot(left, w_s[:, heads, cols].reshape(4 * pw, wide))

            @pl.when(o == 0)
            def _():
                acc[...] = term

            @pl.when(o > 0)
            def _():
                acc[...] += term

            return 0

        lax.fori_loop(0, PAIRS, step, 0)
        st_s[:, cols] = (st_s[:, cols].astype(jnp.float32) - acc[...]).astype(jnp.bfloat16)
        stream_on(n).start()

    def att_relay(o):
        arrive(att_own(o))
        start(att_pass(o))

    for key in ("k", "v", "q", "w", "g", "s"):
        loads[key].start()

    awaited = len(partners) + jnp.where(is_first, 3, 0) + jnp.where(is_relay, 1, 0)
    pl.semaphore_wait(barrier, awaited)
    for f in range(2):
        w_first(RIGHT, f).start()
        w_first(LEFT, f).start()

    @pl.when(has_next)
    def _():
        start(halo())

    for f in range(2):
        w_first(FAR, f).start()

    @pl.when(x > 0)
    def _():
        for s in range(4):
            grad_on(s).start()

    @pl.when(jnp.logical_not(has_prev))
    def _():
        k_s[pl.ds(0, rows), :] = jnp.zeros((rows, width), k_s.dtype)
        v_s[pl.ds(0, rows), :] = jnp.zeros((rows, width), v_s.dtype)

    @pl.when(jnp.logical_not(has_next))
    def _():
        ret_in[...] = jnp.zeros(ret_in.shape, ret_in.dtype)

    fill_bias()
    own_block(LEFT, 0)
    own_block(RIGHT, 0)
    for key in ("k", "v", "q"):
        loads[key].wait()
    w_first(FAR, 0).wait_recv()

    @pl.when(core == 0)
    def _():
        w_up(LEFT, 0, x).start()
        w_up(RIGHT, 0, x).start()

    own_block_on(FAR, 0)
    up_block(LEFT, 0)
    up_block(RIGHT, 0)

    @pl.when(has_prev)
    def _():
        arrive(halo())

    @pl.when(x == 0)
    def _():
        for s in range(4):
            grad_on(s).start()

    forward(0)
    start(att_own(0))
    up_block(FAR, 0)
    own_block(LEFT, 1)
    own_block(RIGHT, 1)
    own_block(FAR, 1)
    forward(1)
    start(att_own(1))
    down_block(LEFT, 0)
    att_relay(0)
    forward(2)
    start(att_own(2))
    down_block(RIGHT, 0)
    att_relay(1)
    forward(3)
    start(att_own(3))
    down_block(FAR, 0)
    far_block(LEFT, 0)
    far_block(RIGHT, 0)
    att_relay(2)
    loads["w"].wait()
    loads["g"].wait()
    mate_blocks(0)
    d_out_terms(0)
    start(far_terms(0))
    start(plain_terms(0))
    att_relay(3)
    up_block(LEFT, 1)
    far_block(FAR, 0)
    down_block(LEFT, 1)
    up_block(RIGHT, 1)
    down_block(RIGHT, 1)
    loads["s"].wait()
    for o in range(1, PAIRS):
        mate_blocks(o, (0,))
    up_block(FAR, 1)
    mate_blocks(1, (1,))
    d_out_terms(1)
    start(far_terms(1))
    start(plain_terms(1))
    for o in range(PAIRS):
        arrive(att_pass(o))
    rebuild(0)
    down_block(FAR, 1)
    merge(0)
    mate_blocks(2, (1,))
    d_out_terms(2)
    start(far_terms(2))
    start(plain_terms(2))
    far_block(LEFT, 1)
    rebuild(1)
    far_block(RIGHT, 1)
    far_block(FAR, 1)
    mate_blocks(3, (1,))
    d_out_terms(3)
    start(far_terms(3))
    start(plain_terms(3))
    merge(1)
    d_out_done(0)
    backward(0)
    merge(2)
    rebuild(2)
    d_out_done(1)
    backward(1)
    merge(3)
    rebuild(3)
    d_out_done(2)
    backward(2)
    relay_on(0)
    d_out_done(3)
    backward(3)
    relay_on(1)
    relay_on(2)

    chip_next = lax.rem(x + core, 4)
    pairs_next = [lax.rem(chip_next + n, 4) for n in (0, 1, 3, 2)]
    for o, p in enumerate(pairs_next):
        @pl.when(has_next)
        def _():
            arrive(back(p))

        cols = pl.ds(pl.multiple_of(p * pw, pw), pw)
        for i, (ref, out) in enumerate(((k_s, dk_hbm), (v_s, dv_hbm))):
            total = mine[i, p] + ret_in[i, p].astype(jnp.float32)
            ref[pl.ds(rows, rows), cols] = total.astype(jnp.bfloat16)
            local(ref.at[pl.ds(rows, rows), cols], out.at[0, :, cols], osem.at[1 + i, o]).start()

    for r in (LEFT, RIGHT, FAR):
        for f in range(2):
            w_first((4 - r) % 4, f).wait_send()
            w_up(r, f, x).wait_send()
            w_down(r, f, x).wait_send()
            w_far(r, f, xs[2] if (r, f) in upward else xs[1]).wait_send()
            for o in range(PAIRS):
                w_mate(r, f, o, core).wait_send()
    for o in range(PAIRS):
        sent(att_own(o))
        sent(att_pass(o))
        sent(far_terms(o))
        sent(plain_terms(o))
        sent(merged_terms(o))
        grad_on(o).wait_send()
        grad_on(o).wait_recv()
        stream_on(o).wait_send()
        stream_on(o).wait_recv()

    @pl.when(has_next)
    def _():
        sent(halo())

    @pl.when(has_prev)
    def _():
        sent(back(xs[3]))

    @pl.when(has_prev & jnp.logical_not(is_first))
    def _():
        for o in range(3):
            sent(back(xs[o]))

    @pl.when(is_first)
    def _():
        for o in range(3):
            sent(to_relay(o))

    @pl.when(is_relay)
    def _():
        sent(from_relay())

    for o, p in enumerate(pairs_next):
        local(dq_s.at[:, pair_rows(o)], dq_hbm.at[0, :, pair_rows(o)], osem.at[0, o]).wait()
        cols = pl.ds(pl.multiple_of(p * pw, pw), pw)
        for i, (ref, out) in enumerate(((k_s, dk_hbm), (v_s, dv_hbm))):
            local(ref.at[pl.ds(rows, rows), cols], out.at[0, :, cols], osem.at[1 + i, o]).wait()


def body(queries, keys, values, stream, grad_stream, out_proj, doc_ids):
    rows, width = queries.shape[1], queries.shape[2]
    shard = stream.shape[2]
    bf, f32 = jnp.bfloat16, jnp.float32
    qb, pw = rows // 2, 2 * HD
    dma = pltpu.SemaphoreType.DMA
    hbm = pl.BlockSpec(memory_space=pl.ANY)
    sizes = (lax.axis_size("ctx"), lax.axis_size("tp"), lax.axis_size("pipe"))
    assert sizes[0] % 8 == 0 and sizes[1] == 4 and rows == WINDOW and width == 8 * HD
    like = lambda x: jax.ShapeDtypeStruct(x.shape, x.dtype)
    return pl.pallas_call(
        functools.partial(kernel, rows, width, shard, *sizes),
        out_shape=(like(queries), like(keys), like(values), like(stream), like(grad_stream)),
        in_specs=[hbm] * 6 + [pl.BlockSpec(memory_space=pltpu.VMEM)],
        out_specs=(hbm,) * 5,
        scratch_shapes=[
            pltpu.VMEM((4, width, shard), bf),
            pltpu.VMEM((rows, shard), bf),
            pltpu.VMEM((rows, width), bf),
            pltpu.VMEM((2 * rows, width), bf),
            pltpu.VMEM((2 * rows, width), bf),
            pltpu.VMEM((rows, shard), bf),
            pltpu.VMEM((PAIRS, 4, pw, rows), bf),
            pltpu.VMEM((4, PAIRS, rows, pw), bf),
            pltpu.VMEM((PAIRS, pw, rows), bf),
            pltpu.VMEM((8, 2, 3 * qb, qb), bf),
            pltpu.VMEM((2, 3 * qb, qb), f32),
            pltpu.VMEM((rows, shard // 4), f32),
            pltpu.VMEM((2, PAIRS, rows, pw), bf),
            pltpu.VMEM((2, PAIRS, rows, pw), bf),
            pltpu.VMEM((2, rows, pw), bf),
            pltpu.VMEM((2, PAIRS, rows, pw), f32),
            pltpu.VMEM((rows, width), bf),
            pltpu.VMEM((PAIRS, pw, qb), bf),
            pltpu.VMEM((PAIRS, pw, qb), bf),
            pltpu.VMEM((PAIRS, pw, rows), bf),
            pltpu.VMEM((PAIRS, pw, rows), bf),
            dma((6,)), dma((3, 4)),
            dma((3, 2)), dma((3, 2)), dma((3, 3, 2)), dma((3, 3, 2)), dma((4, 3, 2)), dma((4, 3, 2)),
            dma((4, 4)), dma((4, 4)),
            dma((2,)), dma((2,)), dma((2, 5)), dma((2, 4)), dma((2, 3)), dma((2,)),
            dma((3, 2, 4)), dma((3, 2, 4)),
            dma((4,)), dma((4,)), dma((4,)), dma((4,)),
        ],
        compiler_params=pltpu.CompilerParams(
            collective_id=0, has_side_effects=True, vmem_limit_bytes=67043328
        ),
    )(queries, keys, values, stream, grad_stream, out_proj, doc_ids)


def solution(mesh):
    spec = P("pipe", "ctx", "tp")
    in_specs = (spec,) * 5 + (P("pipe", "tp", None), P("pipe", None))
    return jax.shard_map(body, mesh=mesh, in_specs=in_specs, out_specs=(spec,) * 5, check_vma=False)
```

```python
import functools
import math

import jax
import jax.numpy as jnp
from jax import lax
from jax.experimental import pallas as pl
from jax.experimental.pallas import tpu as pltpu
from jax.sharding import PartitionSpec as P

HD = 128
WINDOW = 512
NEG = -1e30
MESH = pl.DeviceIdType.MESH
NT = (((1,), (1,)), ((), ()))
OWN, RIGHT, FAR, LEFT = 0, 1, 2, 3
PAIRS = 4


def dot(a, b, dims=(((1,), (0,)), ((), ()))):
    return lax.dot_general(a, b, dims, preferred_element_type=jnp.float32)


def kernel(
    rows, width, shard, ctx_n, tp_n, pipe_n,
    q_hbm, k_hbm, v_hbm, s_hbm, g_hbm, w_hbm, doc_ref,
    dq_hbm, dk_hbm, dv_hbm, ns_hbm, ng_hbm,
    w_s, g_s, q_s, k_s, v_s, st_s, part, att, out_t, prob, bias,
    acc, ret_out, ret_in, relay, mine, dq_s, in_a, in_b, fin_l, fin_r,
    lsem, osem, w1s, w1r, wxs, wxr, wcs, wcr, ats, atr, hs, hr, rts, rtr, rls, rlr, rss, rsr, pgs, pgr, prs, prr,
):
    pipe = lax.axis_index("pipe")
    c = lax.axis_index("ctx")
    z = lax.axis_index("tp")
    nxt, prv = lax.rem(c + 1, ctx_n), lax.rem(c + ctx_n - 1, ctx_n)
    other = lax.rem(pipe + 1, pipe_n)
    has_prev, has_next = c > 0, c < ctx_n - 1
    qb, sub = rows // 2, rows // 4
    kw, pw = 3 * qb, 2 * HD
    row = c // 8
    x, core = lax.rem(c, 8) // 2, lax.rem(c, 2)
    mate = 1 - core
    xs = (x, lax.rem(x + 1, 4), lax.rem(x + 3, 4), lax.rem(x + 2, 4))

    def at_x(chip, side):
        return {"ctx": row * 8 + chip * 2 + side}

    to_z = {d: {"tp": lax.rem(z + d, tp_n)} for d in (RIGHT, FAR, LEFT)}
    x_up, x_down, x_mate = at_x(xs[1], core), at_x(xs[2], core), at_x(x, mate)

    barrier = pltpu.get_barrier_semaphore()
    partners = (*to_z.values(), x_up, x_down, x_mate, {"ctx": nxt}, {"ctx": prv}, {"pipe": other})
    for where in partners:
        pl.semaphore_signal(barrier, inc=1, device_id=where, device_id_type=MESH)

    more_rows = c < ctx_n - 8
    is_first = (lax.rem(c, 8) == 0) & has_prev
    is_relay = (core == 0) & (x < 3) & more_rows
    is_last = (lax.rem(c, 8) == 7) & more_rows
    row_last = {"ctx": row * 8 + 7}
    row_next = {"ctx": lax.rem(row * 8 + 8, ctx_n)}

    @pl.when(is_relay)
    def _():
        pl.semaphore_signal(barrier, inc=1, device_id=row_next, device_id_type=MESH)

    @pl.when(is_last)
    def _():
        for chip in range(3):
            pl.semaphore_signal(barrier, inc=1, device_id=at_x(chip, 0), device_id_type=MESH)

    def local(src, dst, sem):
        return pltpu.make_async_copy(src, dst, sem)

    def remote(src, dst, ssem, rsem, where):
        return pltpu.make_async_remote_copy(
            src_ref=src, dst_ref=dst, send_sem=ssem, recv_sem=rsem,
            device_id=where, device_id_type=MESH,
        )

    def features(d):
        return pl.ds(pl.multiple_of(lax.rem(z + d, tp_n) * shard, shard), shard)

    def block(chip, side):
        return pl.ds(pl.multiple_of((chip * 2 + side) * HD, HD), HD)

    def pair_rows(o):
        return pl.ds(pl.multiple_of(xs[o] * pw, pw), pw)

    loads = {
        "q": local(q_hbm.at[0], q_s, lsem.at[0]),
        "k": local(k_hbm.at[0], k_s.at[pl.ds(rows, rows)], lsem.at[1]),
        "v": local(v_hbm.at[0], v_s.at[pl.ds(rows, rows)], lsem.at[2]),
        "g": local(g_hbm.at[0], g_s, lsem.at[3]),
        "w": local(w_hbm.at[0, :, features(OWN)], w_s.at[OWN], lsem.at[4]),
        "s": local(s_hbm.at[0], st_s, lsem.at[5]),
    }

    part_f = shard // 2

    def w_first(d, f):
        there = (4 - d) % 4
        here = block(x, core)
        start_at = lax.rem(z + d, tp_n) * shard + f * part_f
        cols = pl.ds(pl.multiple_of(start_at, part_f), part_f)
        return remote(
            w_hbm.at[0, here, cols], w_s.at[there, here, pl.ds(f * part_f, part_f)],
            w1s.at[there - 1, f], w1r.at[there - 1, f], to_z[d],
        )

    def w_piece(r, f, chip, side, ssem, rsem, where):
        here = w_s.at[r, block(chip, side), pl.ds(f * part_f, part_f)]
        return remote(here, here, ssem, rsem, where)

    def w_up(r, f, chip):
        return w_piece(r, f, chip, core, wxs.at[0, r - 1, f], wxr.at[0, r - 1, f], x_up)

    def w_down(r, f, chip):
        return w_piece(r, f, chip, core, wxs.at[1, r - 1, f], wxr.at[1, r - 1, f], x_down)

    upward = ((RIGHT, 1), (FAR, 1))

    def w_far(r, f, chip):
        where = x_up if (r, f) in upward else x_down
        return w_piece(r, f, chip, core, wxs.at[2, r - 1, f], wxr.at[2, r - 1, f], where)

    def w_mate(r, f, o, side):
        return w_piece(r, f, xs[o], side, wcs.at[o, r - 1, f], wcr.at[o, r - 1, f], x_mate)

    def own_block(r, f):
        w_first((4 - r) % 4, f).wait_recv()
        own_block_on(r, f)

    def own_block_on(r, f):
        if r == FAR or f == 1:
            w_up(r, f, x).start()
        else:
            @pl.when(core == 1)
            def _():
                w_up(r, f, x).start()

        w_down(r, f, x).start()
        w_mate(r, f, 0, core).start()

    def up_block(r, f):
        w_down(r, f, xs[1]).wait_recv()
        if (r, f) not in upward:
            w_far(r, f, xs[1]).start()
        w_mate(r, f, 1, core).start()

    def down_block(r, f):
        w_up(r, f, xs[2]).wait_recv()
        if (r, f) in upward:
            w_far(r, f, xs[2]).start()
        w_mate(r, f, 2, core).start()

    def far_block(r, f):
        w_far(r, f, xs[3]).wait_recv()
        w_mate(r, f, 3, core).start()

    def mate_blocks(o, halves=(0, 1)):
        for f in halves:
            for r in (LEFT, RIGHT, FAR):
                w_mate(r, f, o, mate).wait_recv()

    lo, hi = pl.ds(0, qb), pl.ds(qb, qb)

    def att_own(o):
        return (
            remote(att.at[OWN, o], att.at[LEFT, o], ats.at[0, o], atr.at[0, o], to_z[RIGHT]),
            remote(att.at[OWN, o], att.at[RIGHT, o], ats.at[1, o], atr.at[1, o], to_z[LEFT]),
        )

    def att_pass(o):
        return (
            remote(att.at[LEFT, o, lo], att.at[FAR, o, lo], ats.at[2, o], atr.at[2, o], to_z[RIGHT]),
            remote(att.at[RIGHT, o, hi], att.at[FAR, o, hi], ats.at[3, o], atr.at[3, o], to_z[LEFT]),
        )

    def far_terms(o):
        return (
            remote(part.at[o, FAR, :, lo], in_a.at[o], rss.at[0, 0, o], rsr.at[0, 0, o], to_z[RIGHT]),
            remote(part.at[o, FAR, :, hi], in_b.at[o], rss.at[0, 1, o], rsr.at[0, 1, o], to_z[LEFT]),
        )

    def plain_terms(o):
        return (
            remote(part.at[o, RIGHT, :, hi], fin_l.at[o, :, hi], rss.at[1, 0, o], rsr.at[1, 0, o], to_z[RIGHT]),
            remote(part.at[o, LEFT, :, lo], fin_r.at[o, :, lo], rss.at[1, 1, o], rsr.at[1, 1, o], to_z[LEFT]),
        )

    def merged_terms(o):
        return (
            remote(part.at[o, RIGHT, :, lo], fin_l.at[o, :, lo], rss.at[2, 0, o], rsr.at[2, 0, o], to_z[RIGHT]),
            remote(part.at[o, LEFT, :, hi], fin_r.at[o, :, hi], rss.at[2, 1, o], rsr.at[2, 1, o], to_z[LEFT]),
        )

    def halo():
        return (
            remote(k_hbm.at[0], k_s.at[pl.ds(0, rows)], hs.at[0], hr.at[0], {"ctx": nxt}),
            remote(v_hbm.at[0], v_s.at[pl.ds(0, rows)], hs.at[1], hr.at[1], {"ctx": nxt}),
        )

    def back(p):
        return tuple(
            remote(ret_out.at[i, p], ret_in.at[i, p], rts.at[i, p], rtr.at[i, p], {"ctx": prv})
            for i in range(2)
        )

    def to_relay(o):
        where = {"ctx": jnp.maximum(row - 1, 0) * 8 + o * 2}
        return tuple(
            remote(ret_out.at[i, xs[o]], relay.at[i], rls.at[i, o], rlr.at[i], where)
            for i in range(2)
        )

    def from_relay():
        p = x + x // 2
        return tuple(
            remote(relay.at[i], ret_in.at[i, p], rts.at[i, 4], rtr.at[i, p], row_last)
            for i in range(2)
        )

    def relay_on(chip):
        @pl.when(is_relay & (x == chip))
        def _():
            arrive(tuple(
                remote(ret_out.at[i, 0], relay.at[i], rls.at[i, 0], rlr.at[i], row_next) for i in range(2)
            ))
            start(from_relay())

    def grad_on(s):
        here = pl.ds(s * sub, sub)
        return remote(g_hbm.at[0, here], ng_hbm.at[0, here], pgs.at[s], pgr.at[s], {"pipe": other})

    wide = shard // 8

    def stream_on(n):
        cols = pl.ds(n * wide, wide)
        return remote(st_s.at[:, cols], ns_hbm.at[0, :, cols], prs.at[n], prr.at[n], {"pipe": other})

    def start(copies):
        for copy in copies:
            copy.start()

    def arrive(copies):
        for copy in copies:
            copy.wait_recv()

    def sent(copies):
        for copy in copies:
            copy.wait_send()

    def fill_bias():
        own_doc = doc_ref[:, pl.ds(pl.multiple_of(c * rows, rows), rows)].astype(jnp.float32)
        old_doc = doc_ref[:, pl.ds(pl.multiple_of(jnp.maximum(c - 1, 0) * rows, rows), rows)].astype(jnp.float32)
        key_doc = jnp.transpose(jnp.broadcast_to(jnp.concatenate([old_doc, own_doc], axis=1), (HD, 2 * rows)))
        a = lax.broadcasted_iota(jnp.int32, (kw, qb), 0)
        b = lax.broadcasted_iota(jnp.int32, (kw, qb), 1)
        for t in range(2):
            seen = (a <= b + rows) & (a > b + (rows - WINDOW))
            seen = seen & ((a + t * qb >= rows) | has_prev)
            columns = jnp.broadcast_to(key_doc[t * qb:t * qb + kw, :1], (kw, qb))
            seen = seen & (columns == own_doc[:, t * qb:(t + 1) * qb])
            bias[t] = jnp.where(seen, 0.0, NEG)

    scaling = HD ** -0.5

    def forward(o):
        def step(i, _):
            cols = pl.ds(pl.multiple_of(xs[o] * pw + i * HD, HD), HD)
            mine_cols = pl.ds(pl.multiple_of(i * HD, HD), HD)
            for t in range(2):
                tokens = pl.ds(t * qb, qb)
                keys = k_s[pl.ds(t * qb, kw), cols]
                values = v_s[pl.ds(t * qb, kw), cols]
                scores = dot(keys, q_s[tokens, cols], NT) + bias[t]
                top = jnp.max(scores, axis=0, keepdims=True)
                exponent = jnp.exp2((scores - top) * (scaling * math.log2(math.e)))
                total = jnp.sum(exponent, axis=0, keepdims=True)
                weights = (exponent * (1.0 / total)).astype(jnp.bfloat16)
                prob[o * 2 + i, t] = weights
                out = dot(jnp.transpose(values), weights)
                out_t[o, mine_cols, tokens] = out.astype(jnp.bfloat16)
                att[OWN, o, tokens, mine_cols] = jnp.transpose(out).astype(jnp.bfloat16)
            return 0

        lax.fori_loop(0, 2, step, 0)

    def d_out_terms(o):
        def step(r, _):
            term = dot(w_s[r, pair_rows(o), :], g_s[...], NT)
            part[o, r] = term.astype(jnp.bfloat16)
            return 0

        lax.fori_loop(0, 4, step, 0)

    def add_into(r, o, cols, extra):
        part[o, r, :, cols] = (
            part[o, r, :, cols].astype(jnp.float32) + extra.astype(jnp.float32)
        ).astype(jnp.bfloat16)

    def merge(o):
        arrive(far_terms(o))
        add_into(RIGHT, o, lo, in_a[o])
        add_into(LEFT, o, hi, in_b[o])
        start(merged_terms(o))

    def d_out_done(o):
        arrive(plain_terms(o))
        arrive(merged_terms(o))
        total = part[o, OWN].astype(jnp.float32) + fin_l[o].astype(jnp.float32) + fin_r[o].astype(jnp.float32)
        part[o, OWN] = total.astype(jnp.bfloat16)

    def backward(o):
        def step(i, _):
            cols = pl.ds(pl.multiple_of(xs[o] * pw + i * HD, HD), HD)
            mine_cols = pl.ds(pl.multiple_of(i * HD, HD), HD)
            d_keys, d_values = [], []
            for t in range(2):
                tokens = pl.ds(t * qb, qb)
                keys = k_s[pl.ds(t * qb, kw), cols]
                values = v_s[pl.ds(t * qb, kw), cols]
                queries = q_s[tokens, cols]
                d_out = part[o, OWN, mine_cols, tokens]
                weights = prob[o * 2 + i, t]
                delta = jnp.sum(
                    d_out.astype(jnp.float32) * out_t[o, mine_cols, tokens].astype(jnp.float32),
                    axis=0, keepdims=True,
                )
                d_prob = dot(values, d_out)
                d_score = (weights.astype(jnp.float32) * (d_prob - delta)).astype(jnp.bfloat16)
                d_values.append(dot(weights, d_out, NT))
                d_keys.append(dot(d_score, queries) * scaling)
                d_query = dot(jnp.transpose(keys), d_score) * scaling
                dq_s[tokens, cols] = jnp.transpose(d_query).astype(jnp.bfloat16)
            for n, (early, late) in enumerate((d_keys, d_values)):
                ret_out[n, xs[o], pl.ds(0, qb), mine_cols] = early[:qb].astype(jnp.bfloat16)
                ret_out[n, xs[o], pl.ds(qb, qb), mine_cols] = (early[qb:2 * qb] + late[:qb]).astype(jnp.bfloat16)
                mine[n, xs[o], pl.ds(0, qb), mine_cols] = early[2 * qb:] + late[qb:2 * qb]
                mine[n, xs[o], pl.ds(qb, qb), mine_cols] = late[2 * qb:]
            return 0

        lax.fori_loop(0, 2, step, 0)

        @pl.when(has_prev if o == 3 else has_prev & jnp.logical_not(is_first))
        def _():
            start(back(xs[o]))

        if o < 3:
            @pl.when(is_first)
            def _():
                start(to_relay(o))

        local(dq_s.at[:, pair_rows(o)], dq_hbm.at[0, :, pair_rows(o)], osem.at[0, o]).start()

    def rebuild(n):
        rebuild_part(2 * n)
        rebuild_part(2 * n + 1)

    def rebuild_part(n):
        cols = pl.ds(n * wide, wide)

        def step(o, _):
            pair = lax.rem(x + o + o // 2 - 2 * (o // 3), 4)
            heads = pl.ds(pl.multiple_of(pair * pw, pw), pw)
            left = jnp.concatenate([att[r, o] for r in range(4)], axis=1)
            term = dot(left, w_s[:, heads, cols].reshape(4 * pw, wide))

            @pl.when(o == 0)
            def _():
                acc[...] = term

            @pl.when(o > 0)
            def _():
                acc[...] += term

            return 0

        lax.fori_loop(0, PAIRS, step, 0)
        st_s[:, cols] = (st_s[:, cols].astype(jnp.float32) - acc[...]).astype(jnp.bfloat16)
        stream_on(n).start()

    def att_relay(o):
        arrive(att_own(o))
        start(att_pass(o))

    for key in ("k", "v", "q", "w", "g", "s"):
        loads[key].start()

    awaited = len(partners) + jnp.where(is_first, 3, 0) + jnp.where(is_relay, 1, 0)
    pl.semaphore_wait(barrier, awaited)
    for f in range(2):
        w_first(RIGHT, f).start()
        w_first(LEFT, f).start()

    @pl.when(has_next)
    def _():
        start(halo())

    for f in range(2):
        w_first(FAR, f).start()

    @pl.when(x > 0)
    def _():
        for s in range(4):
            grad_on(s).start()

    @pl.when(jnp.logical_not(has_prev))
    def _():
        k_s[pl.ds(0, rows), :] = jnp.zeros((rows, width), k_s.dtype)
        v_s[pl.ds(0, rows), :] = jnp.zeros((rows, width), v_s.dtype)

    @pl.when(jnp.logical_not(has_next))
    def _():
        ret_in[...] = jnp.zeros(ret_in.shape, ret_in.dtype)

    fill_bias()
    own_block(LEFT, 0)
    own_block(RIGHT, 0)
    for key in ("k", "v", "q"):
        loads[key].wait()
    w_first(FAR, 0).wait_recv()

    @pl.when(core == 0)
    def _():
        w_up(LEFT, 0, x).start()
        w_up(RIGHT, 0, x).start()

    own_block_on(FAR, 0)
    up_block(LEFT, 0)
    up_block(RIGHT, 0)

    @pl.when(has_prev)
    def _():
        arrive(halo())

    @pl.when(x == 0)
    def _():
        for s in range(4):
            grad_on(s).start()

    forward(0)
    start(att_own(0))
    up_block(FAR, 0)
    own_block(LEFT, 1)
    own_block(RIGHT, 1)
    own_block(FAR, 1)
    forward(1)
    start(att_own(1))
    down_block(LEFT, 0)
    att_relay(0)
    forward(2)
    start(att_own(2))
    down_block(RIGHT, 0)
    att_relay(1)
    forward(3)
    start(att_own(3))
    down_block(FAR, 0)
    far_block(LEFT, 0)
    far_block(RIGHT, 0)
    att_relay(2)
    loads["w"].wait()
    loads["g"].wait()
    mate_blocks(0)
    d_out_terms(0)
    start(far_terms(0))
    start(plain_terms(0))
    att_relay(3)
    up_block(LEFT, 1)
    far_block(FAR, 0)
    down_block(LEFT, 1)
    up_block(RIGHT, 1)
    down_block(RIGHT, 1)
    loads["s"].wait()
    for o in range(1, PAIRS):
        mate_blocks(o, (0,))
    up_block(FAR, 1)
    mate_blocks(1, (1,))
    d_out_terms(1)
    start(far_terms(1))
    start(plain_terms(1))
    for o in range(PAIRS):
        arrive(att_pass(o))
    rebuild(0)
    down_block(FAR, 1)
    merge(0)
    mate_blocks(2, (1,))
    d_out_terms(2)
    start(far_terms(2))
    start(plain_terms(2))
    far_block(LEFT, 1)
    rebuild(1)
    far_block(RIGHT, 1)
    far_block(FAR, 1)
    mate_blocks(3, (1,))
    d_out_terms(3)
    start(far_terms(3))
    start(plain_terms(3))
    merge(1)
    d_out_done(0)
    backward(0)
    merge(2)
    rebuild(2)
    d_out_done(1)
    backward(1)
    merge(3)
    rebuild(3)
    d_out_done(2)
    backward(2)
    relay_on(0)
    relay_on(1)
    d_out_done(3)
    backward(3)
    relay_on(2)

    chip_next = lax.rem(x + core, 4)
    pairs_next = [lax.rem(chip_next + n, 4) for n in (0, 1, 3, 2)]
    for o, p in enumerate(pairs_next):
        @pl.when(has_next)
        def _():
            arrive(back(p))

        cols = pl.ds(pl.multiple_of(p * pw, pw), pw)
        for i, (ref, out) in enumerate(((k_s, dk_hbm), (v_s, dv_hbm))):
            total = mine[i, p] + ret_in[i, p].astype(jnp.float32)
            ref[pl.ds(rows, rows), cols] = total.astype(jnp.bfloat16)
            local(ref.at[pl.ds(rows, rows), cols], out.at[0, :, cols], osem.at[1 + i, o]).start()

    for r in (LEFT, RIGHT, FAR):
        for f in range(2):
            w_first((4 - r) % 4, f).wait_send()
            w_up(r, f, x).wait_send()
            w_down(r, f, x).wait_send()
            w_far(r, f, xs[2] if (r, f) in upward else xs[1]).wait_send()
            for o in range(PAIRS):
                w_mate(r, f, o, core).wait_send()
    for o in range(PAIRS):
        sent(att_own(o))
        sent(att_pass(o))
        sent(far_terms(o))
        sent(plain_terms(o))
        sent(merged_terms(o))
        grad_on(o).wait_send()
        grad_on(o).wait_recv()
        for n in (2 * o, 2 * o + 1):
            stream_on(n).wait_send()
            stream_on(n).wait_recv()

    @pl.when(has_next)
    def _():
        sent(halo())

    @pl.when(has_prev)
    def _():
        sent(back(xs[3]))

    @pl.when(has_prev & jnp.logical_not(is_first))
    def _():
        for o in range(3):
            sent(back(xs[o]))

    @pl.when(is_first)
    def _():
        for o in range(3):
            sent(to_relay(o))

    @pl.when(is_relay)
    def _():
        sent(from_relay())

    for o, p in enumerate(pairs_next):
        local(dq_s.at[:, pair_rows(o)], dq_hbm.at[0, :, pair_rows(o)], osem.at[0, o]).wait()
        cols = pl.ds(pl.multiple_of(p * pw, pw), pw)
        for i, (ref, out) in enumerate(((k_s, dk_hbm), (v_s, dv_hbm))):
            local(ref.at[pl.ds(rows, rows), cols], out.at[0, :, cols], osem.at[1 + i, o]).wait()


def body(queries, keys, values, stream, grad_stream, out_proj, doc_ids):
    rows, width = queries.shape[1], queries.shape[2]
    shard = stream.shape[2]
    bf, f32 = jnp.bfloat16, jnp.float32
    qb, pw = rows // 2, 2 * HD
    dma = pltpu.SemaphoreType.DMA
    hbm = pl.BlockSpec(memory_space=pl.ANY)
    sizes = (lax.axis_size("ctx"), lax.axis_size("tp"), lax.axis_size("pipe"))
    assert sizes[0] % 8 == 0 and sizes[1] == 4 and rows == WINDOW and width == 8 * HD
    like = lambda x: jax.ShapeDtypeStruct(x.shape, x.dtype)
    return pl.pallas_call(
        functools.partial(kernel, rows, width, shard, *sizes),
        out_shape=(like(queries), like(keys), like(values), like(stream), like(grad_stream)),
        in_specs=[hbm] * 6 + [pl.BlockSpec(memory_space=pltpu.VMEM)],
        out_specs=(hbm,) * 5,
        scratch_shapes=[
            pltpu.VMEM((4, width, shard), bf),
            pltpu.VMEM((rows, shard), bf),
            pltpu.VMEM((rows, width), bf),
            pltpu.VMEM((2 * rows, width), bf),
            pltpu.VMEM((2 * rows, width), bf),
            pltpu.VMEM((rows, shard), bf),
            pltpu.VMEM((PAIRS, 4, pw, rows), bf),
            pltpu.VMEM((4, PAIRS, rows, pw), bf),
            pltpu.VMEM((PAIRS, pw, rows), bf),
            pltpu.VMEM((8, 2, 3 * qb, qb), bf),
            pltpu.VMEM((2, 3 * qb, qb), f32),
            pltpu.VMEM((rows, shard // 8), f32),
            pltpu.VMEM((2, PAIRS, rows, pw), bf),
            pltpu.VMEM((2, PAIRS, rows, pw), bf),
            pltpu.VMEM((2, rows, pw), bf),
            pltpu.VMEM((2, PAIRS, rows, pw), f32),
            pltpu.VMEM((rows, width), bf),
            pltpu.VMEM((PAIRS, pw, qb), bf),
            pltpu.VMEM((PAIRS, pw, qb), bf),
            pltpu.VMEM((PAIRS, pw, rows), bf),
            pltpu.VMEM((PAIRS, pw, rows), bf),
            dma((6,)), dma((3, 4)),
            dma((3, 2)), dma((3, 2)), dma((3, 3, 2)), dma((3, 3, 2)), dma((4, 3, 2)), dma((4, 3, 2)),
            dma((4, 4)), dma((4, 4)),
            dma((2,)), dma((2,)), dma((2, 5)), dma((2, 4)), dma((2, 3)), dma((2,)),
            dma((3, 2, 4)), dma((3, 2, 4)),
            dma((4,)), dma((4,)), dma((8,)), dma((8,)),
        ],
        compiler_params=pltpu.CompilerParams(
            collective_id=0, has_side_effects=True, vmem_limit_bytes=67043328
        ),
    )(queries, keys, values, stream, grad_stream, out_proj, doc_ids)


def solution(mesh):
    spec = P("pipe", "ctx", "tp")
    in_specs = (spec,) * 5 + (P("pipe", "tp", None), P("pipe", None))
    return jax.shard_map(body, mesh=mesh, in_specs=in_specs, out_specs=(spec,) * 5, check_vma=False)
```
